32 devices in a mesh: gy: 4 (over x, core), gz: 2 (over y), ga: 4 (over z).
Axes of the slice: x: 2, y: 2, z: 4, core: 2. Of those that a mesh axis runs over, the one named last changes fastest.
Arguments:
- fields: float32 [16, 256, 8, 512], P(None, 'gy', 'gz', 'ga'), may hold values from -6 to 6
- section_start: float32 [16, 256, 8, 512], P(None, 'gy', 'gz', 'ga'), may hold values from -6 to 6
- velocity: float32 [3, 256, 8, 512], P(None, 'gy', 'gz', 'ga'), may hold values from -4 to 4
- diffusivity: float32 [16], replicated, may hold values from 0.02 to 0.2
- reaction: float32 [16, 16], replicated, may hold values from -1.5 to 1.5
- x_factor: bfloat16 [512, 64], replicated, may hold values from -0.25 to 0.25
- y_factor: float32 [256, 64], replicated, may hold values from -6 to 6
Outputs:
- new_fields: float32 [16, 256, 8, 512], P(None, 'gy', 'gz', 'ga')
- x_gram: float32 [512, 512], P(('gy', 'gz'))
- y_products: float32 [8, 256, 64], P(('gz', 'gy'))
The draws below stay inside these ranges and needn't reach their ends.
All inputs are finite; a program needn't handle non-finite values.
Results may differ from the reference program's by a relative error of at most 0.0028.
Values may be sent and summed in bfloat16 or wider, within the bound.
No kernel may reach another device: no remote copies, remote signals or barrier semaphores. Data moves between devices by JAX's collectives and lax.ppermute only.
A program may use at most 64 MiB of HBM per device.

```python
import math
import jax
import jax.numpy as jnp
from jax import lax

V = 16
X = 512
Y = 256
RX = 64
RY = 64
XB = 128
Z = 8


def spiked(result, own_key, source, target, blocks, factor):
    def block_of(axis_at):
        return (jnp.arange(result.shape[axis_at]) // (result.shape[axis_at] // blocks)).reshape((-1,) + (1,) * (result.ndim - 1 - axis_at))

    one_side = jax.random.permutation(own_key, blocks)[block_of(target)]
    far = (block_of(target) + blocks // 2) % blocks
    return jnp.where((block_of(source) == one_side) | (block_of(source) == far), factor * result, result)


def block_levels(stream_key, dims, cuts, least, top_value):
    gain = 1.0
    for dim, parts in cuts:
        steps = jax.random.uniform(jax.random.fold_in(jax.random.fold_in(stream_key, 6), dim), (parts,), jnp.float32, least / len(cuts), top_value / len(cuts))
        gain = gain * jnp.repeat(jnp.exp(steps), dims[dim] // parts).reshape((-1,) + (1,) * (len(dims) - 1 - dim))
    return gain


def normal_values(stream_key, extent, width, most, pieces=(), kind=jnp.bfloat16):
    drawn = width * jax.random.normal(stream_key, extent, jnp.float32)
    if pieces:
        drawn = drawn * block_levels(stream_key, extent, pieces, -0.22, 0.18)
    return jnp.clip(drawn, -most, most).astype(kind)


def gaussian_with(stream_key, shape, spread, reach, cuts, heavy, kind=jnp.bfloat16):
    entries = spread * jax.random.normal(stream_key, shape, jnp.float32)
    if cuts:
        entries = entries * block_levels(stream_key, shape, cuts, -0.22, 0.18)
    return jnp.clip(spiked(entries, jax.random.fold_in(stream_key, 3), *heavy), -reach, reach).astype(kind)


def setup_inputs(seed: int = 0) -> dict:
    key_list = jax.random.split(jax.random.key(seed), 8)
    fields = gaussian_with(key_list[0], (V, Y, Z, X), 1.0, 6.0, ((1, 4), (2, 2), (3, 4)), (2, 3, 4, 2.0), jnp.float32)
    section_start = normal_values(key_list[1], (V, Y, Z, X), 1.0, 6.0, ((1, 4), (2, 2), (3, 4)), jnp.float32)
    velocity = normal_values(key_list[2], (3, Y, Z, X), 1.0, 4.0, ((1, 4), (2, 2), (3, 4)), jnp.float32)
    diffusivity = jnp.clip(jnp.exp(jax.random.uniform(key_list[3], (V,), jnp.float32, math.log(0.02), math.log(0.2))), 0.02, 0.2)
    reaction = normal_values(key_list[4], (V, V), V ** -0.5, 1.5, (), jnp.float32)
    x_factor = normal_values(key_list[5], (X, RX), X ** -0.5, 0.25)
    y_factor = normal_values(key_list[6], (Y, RY), 1.0, 6.0, (), jnp.float32)
    return dict(fields=fields, section_start=section_start, velocity=velocity, diffusivity=diffusivity, reaction=reaction, x_factor=x_factor, y_factor=y_factor)


time_step = 0.4


def transport(values, diffusion, velocity):
    padded = jnp.pad(values, 1)
    center = padded[1:-1, 1:-1, 1:-1]
    y_plus = padded[2:, 1:-1, 1:-1]
    y_minus = padded[:-2, 1:-1, 1:-1]
    z_plus = padded[1:-1, 2:, 1:-1]
    z_minus = padded[1:-1, :-2, 1:-1]
    x_plus = padded[1:-1, 1:-1, 2:]
    x_minus = padded[1:-1, 1:-1, :-2]
    laplace_sum = y_plus + y_minus + z_plus + z_minus + x_plus + x_minus - 6.0 * center
    advection = velocity[0] * (x_plus - x_minus) * 0.5 + velocity[1] * (y_plus - y_minus) * 0.5 + velocity[2] * (z_plus - z_minus) * 0.5
    return diffusion * laplace_sum - advection


def reference(fields, section_start, velocity, diffusivity, reaction, x_factor, y_factor):
    transported = lax.map(lambda packed: transport(packed[0], packed[1], velocity), (fields, diffusivity))
    tendency = transported + jnp.einsum("vw,wyzx->vyzx", reaction, fields, precision=lax.Precision.HIGHEST)
    section_value = 0.75 * section_start + 0.25 * (fields + time_step * tendency)
    x_index = lax.broadcasted_iota(jnp.int32, (1, 1, 1, X), 3)
    new_fields = jnp.where(x_index >= X - XB, fields, section_value)
    snapshot = new_fields.astype(jnp.bfloat16)
    unfolded = snapshot.reshape(V * Y * Z, X)
    x_gram = jnp.dot(unfolded.T, unfolded, preferred_element_type=jnp.float32) / float(V * Y * Z)
    projected = jnp.dot(unfolded, x_factor, preferred_element_type=jnp.float32).astype(jnp.bfloat16)
    projected = jnp.transpose(projected.reshape(V, Y, Z, RX), (1, 2, 0, 3)).reshape(Y, Z, V * RX)

    def per_layer(layer):
        layer_rows = lax.dynamic_index_in_dim(projected, layer, 1, keepdims=False)
        layer_gram = jnp.dot(layer_rows, layer_rows.T, preferred_element_type=jnp.float32) / float(V * RX)
        return jnp.dot(layer_gram, y_factor, precision=lax.Precision.HIGHEST)

    y_products = lax.map(per_layer, jnp.arange(Z, dtype=jnp.int32))
    return new_fields, x_gram, y_products
```

```python
import functools

import jax
import jax.numpy as jnp
from jax import lax
from jax.experimental import pallas as pl
from jax.experimental.pallas import tpu as pltpu
from jax.sharding import PartitionSpec as P

time_step = 0.4
TILE = 32
VMEM = pl.BlockSpec(memory_space=pltpu.VMEM)
SMEM = pl.BlockSpec(memory_space=pltpu.SMEM)
f32, bf16 = jnp.float32, jnp.bfloat16


def shift_pairs(count, step):
    return [(i, i + step) for i in range(count) if 0 <= i + step < count]


def ring_pairs(count, step):
    return [(i, (i + step) % count) for i in range(count)]


def pack_kernel(z_cells, single, flags, f_ref, y_first, y_last, x_first, x_last, *z_refs):
    variables, rows, lanes = f_ref.shape
    y_cells = rows // z_cells
    y_first[...] = f_ref[:, :z_cells, :]
    y_last[...] = f_ref[:, rows - z_cells :, :]
    row = lax.broadcasted_iota(jnp.int32, (8, lanes), 0)
    lane = lax.broadcasted_iota(jnp.int32, (8, lanes), 1)
    pick = jnp.where(
        ((row == 0) & (lane == 0)) | ((row == 1) & (lane == lanes - 1)), 1.0, 0.0
    ).astype(bf16)
    for v in range(variables):
        edges = lax.dot_general(
            pick, f_ref[v].astype(bf16), (((1,), (1,)), ((), ())), preferred_element_type=f32
        )
        x_first[:, v * rows : (v + 1) * rows] = edges[0:1, :]
        x_last[:, v * rows : (v + 1) * rows] = edges[1:2, :]
        if single:
            start = jnp.where(flags[0] == 0, z_cells - 1, 0)
            z_refs[0][v] = f_ref[v, pl.ds(start, y_cells, stride=z_cells), :].astype(bf16)
        else:
            z_refs[0][v] = f_ref[v, pl.ds(0, y_cells, stride=z_cells), :].astype(bf16)
            z_refs[1][v] = f_ref[v, pl.ds(z_cells - 1, y_cells, stride=z_cells), :].astype(bf16)


def stencil_kernel(
    z_cells, parts, flags, diffusion, reaction, f_ref, s_ref, vel_ref, y_lo, y_hi, x_lo, x_hi, z_lo, z_hi,
    new_ref, *rest
):
    snaps, (padded, edge, zface) = rest[:parts], rest[parts:]
    variables, rows, lanes = f_ref.shape
    y_cells = rows // z_cells
    pad = -(-z_cells // 8) * 8
    step = pl.program_id(0)
    tile = new_ref.shape[1]
    has_z_lo, has_z_hi, me, is_buffer = flags[0], flags[1], flags[2], flags[3]

    @pl.when(step == 0)
    def _():
        row = lax.broadcasted_iota(jnp.int32, (8, lanes), 0)
        lane = lax.broadcasted_iota(jnp.int32, (8, lanes), 1)
        put = jnp.where(
            ((row == 0) & (lane == 0)) | ((row == 1) & (lane == lanes - 1)), 1.0, 0.0
        ).astype(bf16)
        side = lax.broadcasted_iota(jnp.int32, (8, rows), 0)
        for v in range(variables):
            padded[v, pad : pad + rows, :] = f_ref[v]
            padded[v, pad - z_cells : pad, :] = y_lo[v]
            padded[v, pad + rows : pad + rows + z_cells, :] = y_hi[v]
            low = jnp.broadcast_to(x_lo[:, v * rows : (v + 1) * rows], (8, rows))
            high = jnp.broadcast_to(x_hi[:, v * rows : (v + 1) * rows], (8, rows))
            both = jnp.where(side == 0, low, jnp.where(side == 1, high, 0.0)).astype(bf16)
            edge[v] = lax.dot_general(both, put, (((0,), (0,)), ((), ())), preferred_element_type=f32)
            zface[v, pl.ds(0, y_cells, stride=z_cells), :] = jnp.where(has_z_lo != 0, z_lo[v].astype(f32), 0.0)
            zface[v, pl.ds(z_cells - 1, y_cells, stride=z_cells), :] = jnp.where(
                has_z_hi != 0, z_hi[v].astype(f32), 0.0
            )

    base = step * tile
    lane = lax.broadcasted_iota(jnp.int32, (tile, lanes), 1)
    z_at = lax.rem(lax.broadcasted_iota(jnp.int32, (tile, lanes), 0), z_cells)
    group = variables // parts
    v_x = vel_ref[0] * 0.5
    v_y = vel_ref[1] * 0.5
    v_z = vel_ref[2] * 0.5
    for part in range(parts):
        target = lax.rem(me + part, parts)
        for j in range(group):
            v = target * group + j
            center = padded[v, pl.ds(base + pad, tile), :]
            y_minus = padded[v, pl.ds(base + pad - z_cells, tile), :]
            y_plus = padded[v, pl.ds(base + pad + z_cells, tile), :]
            face = zface[v, pl.ds(base, tile), :]
            z_minus = jnp.where(z_at == 0, face, padded[v, pl.ds(base + pad - 1, tile), :])
            z_plus = jnp.where(z_at == z_cells - 1, face, padded[v, pl.ds(base + pad + 1, tile), :])
            sides = edge[v, pl.ds(base, tile), :]
            x_minus = jnp.where(lane == 0, sides, pltpu.roll(center, 1, 1))
            x_plus = jnp.where(lane == lanes - 1, sides, pltpu.roll(center, lanes - 1, 1))
            laplace = y_plus + y_minus + z_plus + z_minus + x_plus + x_minus - 6.0 * center
            total = diffusion[v] * laplace - (
                v_x * (x_plus - x_minus) + v_y * (y_plus - y_minus) + v_z * (z_plus - z_minus)
            )
            for w in range(variables):
                total = total + reaction[v, w] * padded[w, pl.ds(base + pad, tile), :]
            value = 0.75 * s_ref[v] + 0.25 * (center + time_step * total)
            value = jnp.where(is_buffer != 0, center, value)
            new_ref[v] = value
            snaps[part][j] = value.astype(bf16)


def gram_kernel(z_cells, parts, flags, xf_ref, *refs):
    pieces, (gram_ref, proj_ref, wide, proj) = refs[:parts], refs[parts:]
    group, rows, lanes = pieces[0].shape
    y_cells = rows // z_cells
    rank = xf_ref.shape[0]
    me = flags[2]
    for part in range(parts):
        source = lax.rem(me - part + parts, parts)
        at = pl.multiple_of(source * lanes, lanes)
        for j in range(group):
            wide[j * rows : (j + 1) * rows, pl.ds(at, lanes)] = pieces[part][j]
    data = wide[...]
    gram = lax.dot_general(data, data, (((0,), (0,)), ((), ())), preferred_element_type=f32)
    gram_ref[...] = gram.astype(bf16)
    proj[...] = lax.dot_general(
        data, xf_ref[...], (((1,), (1,)), ((), ())), preferred_element_type=f32
    )
    for z in range(z_cells):
        cols = [proj[pl.ds(j * rows + z, y_cells, stride=z_cells), :] for j in range(group)]
        proj_ref[z] = jnp.concatenate(cols, axis=1).astype(bf16)


def layer_kernel(y_scale, x_scale, gram_ref, full_ref, yf_ref, out_ref):
    owners, own_rows, width = gram_ref.shape
    total = gram_ref[0].astype(f32)
    for i in range(1, owners):
        total = total + gram_ref[i].astype(f32)
    layers = full_ref.shape[1]
    rank = yf_ref.shape[0]
    if own_rows != rank:
        out_ref[...] = jnp.zeros_like(out_ref)
    out_ref[:own_rows, :width] = (total * x_scale).astype(bf16)
    y_size = yf_ref.shape[1]
    for layer in range(layers):
        m = full_ref[:, layer].reshape(y_size, full_ref.shape[3])
        y_gram = lax.dot_general(m, m, (((1,), (1,)), ((), ())), preferred_element_type=f32) * y_scale
        prod = lax.dot_general(
            yf_ref[...], y_gram, (((1,), (0,)), ((), ())), preferred_element_type=f32,
            precision=lax.Precision.HIGHEST,
        )
        out_ref[:rank, width + layer * y_size : width + (layer + 1) * y_size] = prod.astype(bf16)


def last_kernel(width, parts, *refs):
    pieces, (gram_ref, prod_ref) = refs[:parts], refs[parts:]
    total = pieces[0][...].astype(f32)
    for i in range(1, parts):
        total = total + pieces[i][...].astype(f32)
    gram_ref[...] = total[: gram_ref.shape[0], :width]
    layers, rank, y_size = prod_ref.shape
    for layer in range(layers):
        prod_ref[layer] = total[:rank, width + layer * y_size : width + (layer + 1) * y_size]


def call(kernel, out_shapes, in_specs, scratch=(), name=None, flops=0, moved=0):
    return pl.pallas_call(
        kernel,
        out_shape=out_shapes,
        in_specs=in_specs,
        out_specs=[VMEM] * len(out_shapes),
        scratch_shapes=list(scratch),
        name=name,
        cost_estimate=pl.CostEstimate(flops=flops, bytes_accessed=moved, transcendentals=0),
        compiler_params=pltpu.CompilerParams(vmem_limit_bytes=60 * 1024 * 1024),
    )


def shards(fields, section_start, velocity, diffusivity, reaction, x_factor, y_factor):
    sds = jax.ShapeDtypeStruct
    variables, y_cells, z_cells, lanes = fields.shape
    rows = y_cells * z_cells
    n_y, n_z, n_a = (lax.axis_size(a) for a in ("gy", "gz", "ga"))
    g_z, g_a = lax.axis_index("gz"), lax.axis_index("ga")
    single = n_z == 2
    f = fields.reshape(variables, rows, lanes)
    s = section_start.reshape(variables, rows, lanes)
    vel = velocity.reshape(3, rows, lanes)
    x_size = n_a * lanes
    y_size = n_y * y_cells
    rank = x_factor.shape[1]
    group = variables // n_a

    packed = call(
        functools.partial(pack_kernel, z_cells, single),
        [sds((variables, z_cells, lanes), f32)] * 2
        + [sds((1, variables * rows), f32)] * 2
        + [sds((variables, y_cells, lanes), bf16)] * (1 if single else 2),
        [SMEM, VMEM],
        name="pack",
        moved=f.size * 4,
    )(g_z.reshape(1).astype(jnp.int32), f)
    y_first, y_last, x_first, x_last = packed[:4]
    if single:
        face = lax.ppermute(packed[4], "gz", [(0, 1), (1, 0)])
        z_lo = z_hi = face
    else:
        z_hi = lax.ppermute(packed[4], "gz", shift_pairs(n_z, -1))
        z_lo = lax.ppermute(packed[5], "gz", shift_pairs(n_z, 1))
    x_lo = lax.ppermute(x_last, "ga", shift_pairs(n_a, 1))
    x_hi = lax.ppermute(x_first, "ga", shift_pairs(n_a, -1))
    y_lo = lax.ppermute(y_last, "gy", shift_pairs(n_y, 1))
    y_hi = lax.ppermute(y_first, "gy", shift_pairs(n_y, -1))

    flags = jnp.stack([g_z > 0, g_z < n_z - 1, g_a, g_a == n_a - 1]).astype(jnp.int32)
    pad = -(-z_cells // 8) * 8
    tile = TILE

    def by_rows(lead):
        return pl.BlockSpec((lead, tile, lanes), lambda i: (0, i, 0))

    def whole(*shape):
        return pl.BlockSpec(shape, lambda i: (0,) * len(shape))

    results = pl.pallas_call(
        functools.partial(stencil_kernel, z_cells, n_a),
        grid=(rows // tile,),
        out_shape=[sds((variables, rows, lanes), f32)] + [sds((group, rows, lanes), bf16)] * n_a,
        in_specs=[
            SMEM, SMEM, SMEM,
            whole(variables, rows, lanes),
            by_rows(variables),
            by_rows(3),
            whole(variables, z_cells, lanes),
            whole(variables, z_cells, lanes),
            whole(1, variables * rows),
            whole(1, variables * rows),
            whole(variables, y_cells, lanes),
            whole(variables, y_cells, lanes),
        ],
        out_specs=[by_rows(variables)] + [by_rows(group)] * n_a,
        scratch_shapes=[
            pltpu.VMEM((variables, rows + 2 * pad, lanes), f32),
            pltpu.VMEM((variables, rows, lanes), f32),
            pltpu.VMEM((variables, rows, lanes), f32),
        ],
        name="stencil",
        compiler_params=pltpu.CompilerParams(vmem_limit_bytes=60 * 1024 * 1024),
    )(flags, diffusivity, reaction, f, s, vel, y_lo, y_hi, x_lo, x_hi, z_lo, z_hi)
    new_fields, snaps = results[0], results[1:]

    pieces = [snaps[0]] + [
        lax.ppermute(snaps[k], "ga", ring_pairs(n_a, k)) for k in range(1, n_a)
    ]
    gram, proj = call(
        functools.partial(gram_kernel, z_cells, n_a),
        [sds((x_size, x_size), bf16), sds((z_cells, y_cells, group * rank), bf16)],
        [SMEM] + [VMEM] * (n_a + 1),
        scratch=[pltpu.VMEM((group * rows, x_size), bf16), pltpu.VMEM((group * rows, rank), f32)],
        name="gram",
    )(flags, x_factor.T, *pieces)
    owners = n_y * n_z
    gram = gram.reshape(owners, x_size // owners, x_size)
    full = lax.all_to_all(
        proj.reshape(n_y, z_cells // n_y, y_cells, group * rank), "gy", split_axis=0, concat_axis=0, tiled=True
    )
    gram = lax.all_to_all(gram, ("gy", "gz"), split_axis=0, concat_axis=0, tiled=True)
    layers = z_cells // n_y
    payload = call(
        functools.partial(
            layer_kernel, 1.0 / (variables * rank), 1.0 / (variables * rows * owners)
        ),
        [sds((max(x_size // owners, y_factor.shape[1]), x_size + layers * y_size), bf16)],
        [VMEM] * 3,
        name="layer",
    )(gram, full, y_factor.T)[0]
    payloads = [payload] + [lax.ppermute(payload, "ga", ring_pairs(n_a, k)) for k in range(1, n_a)]
    x_gram, products = call(
        functools.partial(last_kernel, x_size, n_a),
        [sds((x_size // owners, x_size), f32), sds((layers, y_factor.shape[1], y_size), f32)],
        [VMEM] * n_a,
        name="last",
    )(*payloads)
    return (
        new_fields.reshape(fields.shape),
        x_gram,
        jnp.swapaxes(products, 1, 2),
    )


def solution(mesh):
    block = P(None, "gy", "gz", "ga")
    in_specs = (block, block, block, P(), P(), P(), P())
    out_specs = (block, P(("gy", "gz"), None), P(("gz", "gy"), None, None))
    return jax.shard_map(shards, mesh=mesh, in_specs=in_specs, out_specs=out_specs, check_vma=False)
```

```python
import functools

import jax
import jax.numpy as jnp
from jax import lax
from jax.experimental import pallas as pl
from jax.experimental.pallas import tpu as pltpu
from jax.sharding import PartitionSpec as P

time_step = 0.4
old_share, new_share = 0.75, 0.25
TILE = 32
SUB = 16
CHUNKS = 2
VMEM = pl.BlockSpec(memory_space=pltpu.VMEM)
SMEM = pl.BlockSpec(memory_space=pltpu.SMEM)
ANY = pl.BlockSpec(memory_space=pl.ANY)
f32, bf16 = jnp.float32, jnp.bfloat16
sds = jax.ShapeDtypeStruct
MIB = 1024 * 1024


def shift_pairs(count, step):
    return [(i, i + step) for i in range(count) if 0 <= i + step < count]


def ring_pairs(count, step):
    return [(i, (i + step) % count) for i in range(count)]


def corner_mask(lanes):
    row = lax.broadcasted_iota(jnp.int32, (8, lanes), 0)
    lane = lax.broadcasted_iota(jnp.int32, (8, lanes), 1)
    return jnp.where(
        ((row == 0) & (lane == 0)) | ((row == 1) & (lane == lanes - 1)), 1.0, 0.0
    ).astype(bf16)


def pack_kernel(z_cells, single, flags, f_ref, y_first, y_last, x_first, x_last, *z_refs):
    variables, rows, lanes = f_ref.shape
    y_cells = rows // z_cells
    pick = corner_mask(lanes)
    for v in range(variables):
        if single:
            start = jnp.where(flags[0] == 0, z_cells - 1, 0)
            z_refs[0][v] = f_ref[v, pl.ds(start, y_cells, stride=z_cells), :].astype(bf16)
        else:
            z_refs[0][v] = f_ref[v, pl.ds(0, y_cells, stride=z_cells), :].astype(bf16)
            z_refs[1][v] = f_ref[v, pl.ds(z_cells - 1, y_cells, stride=z_cells), :].astype(bf16)
        edges = lax.dot_general(
            pick, f_ref[v].astype(bf16), (((1,), (1,)), ((), ())), preferred_element_type=f32
        )
        x_first[:, v * rows : (v + 1) * rows] = edges[0:1, :]
        x_last[:, v * rows : (v + 1) * rows] = edges[1:2, :]
        y_first[v] = f_ref[v, :z_cells, :]
        y_last[v] = f_ref[v, rows - z_cells :, :]


def mix_kernel(r_ref, after, out_ref):
    count = r_ref.shape[0]
    size = out_ref.shape[0]
    spread = jnp.where(
        lax.broadcasted_iota(jnp.int32, (size, count), 0) // SUB
        == lax.broadcasted_iota(jnp.int32, (size, count), 1),
        1.0,
        0.0,
    ).astype(bf16)
    scaled = (r_ref[...] * (new_share * time_step)).astype(bf16)
    left = lax.dot_general(spread, scaled, (((1,), (0,)), ((), ())), preferred_element_type=f32)
    both = lax.dot_general(
        left.astype(bf16), spread, (((1,), (1,)), ((), ())), preferred_element_type=f32
    )
    row = lax.broadcasted_iota(jnp.int32, (size, size), 0)
    col = lax.broadcasted_iota(jnp.int32, (size, size), 1)
    out_ref[...] = jnp.where(row % SUB == col % SUB, both, 0.0).astype(bf16)


def stencil_kernel(
    z_cells, parts, first_row, chunk, has_prior, flags, diffusion, f_hbm, s_ref, vel_ref, mix_ref,
    y_lo, y_hi, x_lo, x_hi, z_lo, z_hi, *rest
):
    rest = rest[1:] if has_prior else rest
    new_ref, rest = rest[0], rest[1:]
    snaps, (padded, edge, zface, react, sem) = rest[:parts], rest[parts:]
    variables, rows, lanes = f_hbm.shape
    pad = -(-z_cells // 8) * 8
    low = max(first_row - pad, 0)
    high = min(first_row + chunk + pad, rows)
    step = pl.program_id(0)
    tile = new_ref.shape[1]
    has_z_lo, has_z_hi, me, is_buffer = flags[0], flags[1], flags[2], flags[3]

    @pl.when(step == 0)
    def _():
        load = pltpu.make_async_copy(
            f_hbm.at[:, pl.ds(low, high - low), :],
            padded.at[:, pl.ds(low - first_row + pad, high - low), :],
            sem,
        )
        load.start()
        put = corner_mask(lanes)
        side = lax.broadcasted_iota(jnp.int32, (8, chunk), 0)
        y_count = chunk // z_cells
        y_from = first_row // z_cells
        for v in range(variables):
            at = v * rows + first_row
            first = jnp.broadcast_to(x_lo[:, at : at + chunk], (8, chunk))
            second = jnp.broadcast_to(x_hi[:, at : at + chunk], (8, chunk))
            both = jnp.where(side == 0, first, jnp.where(side == 1, second, 0.0)).astype(bf16)
            edge[v] = lax.dot_general(both, put, (((0,), (0,)), ((), ())), preferred_element_type=f32)
            zface[v, pl.ds(0, y_count, stride=z_cells), :] = jnp.where(
                has_z_lo != 0, z_lo[v, y_from : y_from + y_count, :].astype(f32), 0.0
            )
            zface[v, pl.ds(z_cells - 1, y_count, stride=z_cells), :] = jnp.where(
                has_z_hi != 0, z_hi[v, y_from : y_from + y_count, :].astype(f32), 0.0
            )
        load.wait()
        if first_row == 0:
            padded[:, pad - z_cells : pad, :] = y_lo[...]
        if first_row + chunk == rows:
            padded[:, pad + chunk : pad + chunk + z_cells, :] = y_hi[...]

    base = pl.multiple_of(step * tile, tile)
    blocks = []
    for sub in range(tile // SUB):
        blocks.append(
            jnp.concatenate(
                [padded[w, pl.ds(base + pad + sub * SUB, SUB), :].astype(bf16) for w in range(variables)],
                axis=0,
            )
        )
    react[...] = jnp.dot(mix_ref[...], jnp.concatenate(blocks, axis=1), preferred_element_type=f32)

    rate = new_share * time_step
    lane = lax.broadcasted_iota(jnp.int32, (tile, lanes), 1)
    z_at = lax.rem(lax.broadcasted_iota(jnp.int32, (tile, lanes), 0), z_cells)
    group = variables // parts
    v_x = vel_ref[0] * (0.5 * rate)
    v_y = vel_ref[1] * (0.5 * rate)
    v_z = vel_ref[2] * (0.5 * rate)
    for part in range(parts):
        target = lax.rem(me + part, parts)
        for j in range(group):
            v = target * group + j
            spread = diffusion[v] * rate
            center = padded[v, pl.ds(base + pad, tile), :]
            y_minus = padded[v, pl.ds(base + pad - z_cells, tile), :]
            y_plus = padded[v, pl.ds(base + pad + z_cells, tile), :]
            face = zface[v, pl.ds(base, tile), :]
            z_minus = jnp.where(z_at == 0, face, padded[v, pl.ds(base + pad - 1, tile), :])
            z_plus = jnp.where(z_at == z_cells - 1, face, padded[v, pl.ds(base + pad + 1, tile), :])
            sides = edge[v, pl.ds(base, tile), :]
            x_minus = jnp.where(lane == 0, sides, pltpu.roll(center, 1, 1))
            x_plus = jnp.where(lane == lanes - 1, sides, pltpu.roll(center, lanes - 1, 1))
            mixed = jnp.concatenate(
                [
                    react[pl.ds(pl.multiple_of(v * SUB, SUB), SUB), sub * lanes : (sub + 1) * lanes]
                    for sub in range(tile // SUB)
                ],
                axis=0,
            )
            around = (y_plus + y_minus) + (z_plus + z_minus) + (x_plus + x_minus)
            carried = v_x * (x_plus - x_minus) + v_y * (y_plus - y_minus) + v_z * (z_plus - z_minus)
            value = (
                old_share * s_ref[v]
                + (new_share - 6.0 * spread) * center
                + (spread * around - carried)
                + mixed
            )
            value = jnp.where(is_buffer != 0, center, value)
            new_ref[v] = value
            snaps[part][j] = value.astype(bf16)


def gather_rows(parts, me, pieces, wide):
    group, rows, lanes = pieces[0].shape
    for part in range(parts):
        source = lax.rem(me - part + parts, parts)
        at = pl.multiple_of(source * lanes, lanes)
        for j in range(group):
            wide[j * rows : (j + 1) * rows, pl.ds(at, lanes)] = pieces[part][j]


def project(z_cells, group, rows, xf_ref, wide, proj, store):
    y_cells = rows // z_cells
    proj[...] = lax.dot_general(
        wide[...], xf_ref[...], (((1,), (1,)), ((), ())), preferred_element_type=f32
    )
    for z in range(z_cells):
        cols = [proj[pl.ds(j * rows + z, y_cells, stride=z_cells), :] for j in range(group)]
        store(z, jnp.concatenate(cols, axis=1).astype(bf16))


def part_gram_kernel(z_cells, parts, has_prior, flags, xf_ref, *refs):
    pieces, refs = refs[:parts], refs[parts:]
    if has_prior:
        prior, refs = refs[0], refs[1:]
    gram_ref, proj_ref, wide, proj = refs
    group, rows, lanes = pieces[0].shape
    gather_rows(parts, flags[2], pieces, wide)
    data = wide[...]
    gram = lax.dot_general(data, data, (((0,), (0,)), ((), ())), preferred_element_type=f32)
    gram_ref[...] = prior[...] + gram if has_prior else gram

    def store(z, value):
        proj_ref[z] = value

    project(z_cells, group, rows, xf_ref, wide, proj, store)


def last_gram_kernel(z_cells, parts, n_y, n_z, priors, flags, xf_ref, *refs):
    pieces, refs = refs[:parts], refs[parts:]
    prior, refs = refs[0], refs[1:]
    prior_proj, refs = refs[:priors], refs[priors:]
    outs, (wide, proj, gram, full) = refs[: n_y * n_z], refs[n_y * n_z :]
    group, rows, lanes = pieces[0].shape
    me, my_y, my_z = flags[2], flags[4], flags[5]
    gather_rows(parts, me, pieces, wide)
    y_cells = rows // z_cells

    def store(z, value):
        full[z, priors * y_cells : (priors + 1) * y_cells, :] = value

    project(z_cells, group, rows, xf_ref, wide, proj, store)
    for i in range(priors):
        full[:, i * y_cells : (i + 1) * y_cells, :] = prior_proj[i][...]
    data = wide[...]
    gram[...] = prior[...] + lax.dot_general(
        data, data, (((0,), (0,)), ((), ())), preferred_element_type=f32
    )
    own = gram.shape[0] // (n_y * n_z)
    width = gram.shape[1]
    layers = z_cells // n_y
    cols = full.shape[2]
    for d_y in range(n_y):
        for d_z in range(n_z):
            out = outs[d_y * n_z + d_z]
            y_to, z_to = lax.rem(my_y + d_y, n_y), lax.rem(my_z + d_z, n_z)
            at = pl.multiple_of((y_to * n_z + z_to) * own, own)
            out[:own, :width] = gram[pl.ds(at, own), :].astype(bf16)
            if d_z == 0:
                for layer in range(layers):
                    out[: full.shape[1], width + layer * cols : width + (layer + 1) * cols] = full[
                        y_to * layers + layer
                    ]


def layer_kernel(n_y, n_z, own, layers, y_scale, x_scale, flags, yf_ref, *refs):
    pieces, (out_ref, m_ref) = refs[: n_y * n_z], refs[n_y * n_z :]
    rank, y_size = yf_ref.shape
    y_cells = y_size // n_y
    width = pieces[0].shape[1] if n_z > 1 else 0
    cols = m_ref.shape[2]
    width = pieces[0].shape[1] - layers * cols
    my_y = flags[4]
    for d_y in range(n_y):
        source = lax.rem(my_y - d_y + n_y, n_y)
        at = pl.multiple_of(source * y_cells, y_cells)
        for layer in range(layers):
            m_ref[layer, pl.ds(at, y_cells), :] = pieces[d_y * n_z][
                :y_cells, width + layer * cols : width + (layer + 1) * cols
            ]
    for layer in range(layers):
        m = m_ref[layer]
        y_gram = lax.dot_general(m, m, (((1,), (1,)), ((), ())), preferred_element_type=f32) * y_scale
        prod = lax.dot_general(
            yf_ref[...], y_gram, (((1,), (0,)), ((), ())), preferred_element_type=f32,
            precision=lax.Precision.HIGHEST,
        )
        if own != rank:
            out_ref[...] = jnp.zeros_like(out_ref)
        out_ref[:rank, width + layer * y_size : width + (layer + 1) * y_size] = prod.astype(bf16)
    total = pieces[0][:own, :width].astype(f32)
    for i in range(1, n_y * n_z):
        total = total + pieces[i][:own, :width].astype(f32)
    out_ref[:own, :width] = (total * x_scale).astype(bf16)


def last_kernel(width, parts, *refs):
    pieces, (gram_ref, prod_ref) = refs[:parts], refs[parts:]
    total = pieces[0][...].astype(f32)
    for i in range(1, parts):
        total = total + pieces[i][...].astype(f32)
    gram_ref[...] = total[: gram_ref.shape[0], :width]
    layers, rank, y_size = prod_ref.shape
    for layer in range(layers):
        prod_ref[layer] = total[:rank, width + layer * y_size : width + (layer + 1) * y_size]


def call(kernel, out_shapes, in_specs, scratch=(), name=None, limit=16, flops=0, moved=0):
    return pl.pallas_call(
        kernel,
        out_shape=out_shapes,
        in_specs=in_specs,
        out_specs=[VMEM] * len(out_shapes),
        scratch_shapes=list(scratch),
        name=name,
        cost_estimate=pl.CostEstimate(flops=flops, bytes_accessed=moved, transcendentals=0),
        compiler_params=pltpu.CompilerParams(vmem_limit_bytes=limit * MIB),
    )


def shards(fields, section_start, velocity, diffusivity, reaction, x_factor, y_factor):
    variables, y_cells, z_cells, lanes = fields.shape
    rows = y_cells * z_cells
    n_y, n_z, n_a = (lax.axis_size(a) for a in ("gy", "gz", "ga"))
    g_y, g_z, g_a = (lax.axis_index(a) for a in ("gy", "gz", "ga"))
    single = n_z == 2
    f = fields.reshape(variables, rows, lanes)
    s = section_start.reshape(variables, rows, lanes)
    vel = velocity.reshape(3, rows, lanes)
    x_size = n_a * lanes
    y_size = n_y * y_cells
    rank, y_rank = x_factor.shape[1], y_factor.shape[1]
    group = variables // n_a
    owners = n_y * n_z
    own = x_size // owners
    layers = z_cells // n_y
    chunk = rows // CHUNKS
    pad = -(-z_cells // 8) * 8
    tile = TILE
    flags = jnp.stack([g_z > 0, g_z < n_z - 1, g_a, g_a == n_a - 1, g_y, g_z]).astype(jnp.int32)

    def lead(count, *tail):
        return pl.BlockSpec((count,) + tail, lambda i: (i,) + (0,) * len(tail))

    step_v = group
    packed = pl.pallas_call(
        functools.partial(pack_kernel, z_cells, single),
        grid=(variables // step_v,),
        out_shape=[sds((variables, z_cells, lanes), f32)] * 2
        + [sds((1, variables * rows), f32)] * 2
        + [sds((variables, y_cells, lanes), bf16)] * (1 if single else 2),
        in_specs=[SMEM, lead(step_v, rows, lanes)],
        out_specs=[lead(step_v, z_cells, lanes)] * 2
        + [pl.BlockSpec((1, step_v * rows), lambda i: (0, i))] * 2
        + [lead(step_v, y_cells, lanes)] * (1 if single else 2),
        name="pack",
        compiler_params=pltpu.CompilerParams(vmem_limit_bytes=12 * MIB),
    )(g_z.reshape(1).astype(jnp.int32), f)
    y_first, y_last, x_first, x_last = packed[:4]
    if single:
        face = lax.ppermute(packed[4], "gz", [(0, 1), (1, 0)])
        z_lo = z_hi = face
    else:
        z_hi = lax.ppermute(packed[4], "gz", shift_pairs(n_z, -1))
        z_lo = lax.ppermute(packed[5], "gz", shift_pairs(n_z, 1))
    x_lo = lax.ppermute(x_last, "ga", shift_pairs(n_a, 1))
    x_hi = lax.ppermute(x_first, "ga", shift_pairs(n_a, -1))
    y_lo = lax.ppermute(y_last, "gy", shift_pairs(n_y, 1))
    y_hi = lax.ppermute(y_first, "gy", shift_pairs(n_y, -1))
    mix = call(
        mix_kernel, [sds((variables * SUB, variables * SUB), bf16)], [VMEM, ANY], name="mix", limit=8
    )(reaction, x_first)[0]

    def whole(*shape):
        return pl.BlockSpec(shape, lambda i: (0,) * len(shape))

    def stencil(index, prior):
        first = index * (chunk // tile)

        def by_rows(count):
            return pl.BlockSpec((count, tile, lanes), lambda i: (0, i + first, 0))

        return pl.pallas_call(
            functools.partial(stencil_kernel, z_cells, n_a, index * chunk, chunk, prior is not None),
            grid=(chunk // tile,),
            out_shape=[sds((variables, rows, lanes), f32)] + [sds((group, chunk, lanes), bf16)] * n_a,
            in_specs=[
                SMEM, SMEM, ANY,
                by_rows(variables),
                by_rows(3),
                whole(variables * SUB, variables * SUB),
                whole(variables, z_cells, lanes),
                whole(variables, z_cells, lanes),
                whole(1, variables * rows),
                whole(1, variables * rows),
                whole(variables, y_cells, lanes),
                whole(variables, y_cells, lanes),
            ]
            + ([] if prior is None else [ANY]),
            out_specs=[by_rows(variables)]
            + [pl.BlockSpec((group, tile, lanes), lambda i: (0, i, 0))] * n_a,
            scratch_shapes=[
                pltpu.VMEM((variables, chunk + 2 * pad, lanes), f32),
                pltpu.VMEM((variables, chunk, lanes), f32),
                pltpu.VMEM((variables, chunk, lanes), f32),
                pltpu.VMEM((variables * SUB, tile // SUB * lanes), f32),
                pltpu.SemaphoreType.DMA,
            ],
            input_output_aliases={} if prior is None else {12: 0},
            name="stencil",
            compiler_params=pltpu.CompilerParams(vmem_limit_bytes=24 * MIB),
        )(flags, diffusivity, f, s, vel, mix, y_lo, y_hi, x_lo, x_hi, z_lo, z_hi, *([] if prior is None else [prior]))

    def exchange(snaps):
        return [snaps[0]] + [lax.ppermute(snaps[k], "ga", ring_pairs(n_a, k)) for k in range(1, n_a)]

    new_fields, chunks = None, []
    for index in range(CHUNKS):
        results = stencil(index, new_fields)
        new_fields = results[0]
        chunks.append(exchange(results[1:]))

    scratch = [pltpu.VMEM((group * chunk, x_size), bf16), pltpu.VMEM((group * chunk, rank), f32)]
    y_part = chunk // z_cells
    gram, projs = None, []
    direct = owners <= 8
    for index in range(CHUNKS - 1 if direct else CHUNKS):
        gram, proj = call(
            functools.partial(part_gram_kernel, z_cells, n_a, gram is not None),
            [sds((x_size, x_size), f32), sds((z_cells, y_part, group * rank), bf16)],
            [SMEM] + [VMEM] * (n_a + 1 + (gram is not None)),
            scratch=scratch,
            name="gram",
        )(flags, x_factor.T, *chunks[index], *([] if gram is None else [gram]))
        projs.append(proj)
    cols = layers * group * rank
    piece_rows = max(own, y_cells)
    if direct:
        pieces = call(
            functools.partial(last_gram_kernel, z_cells, n_a, n_y, n_z, len(projs)),
            [
                sds((piece_rows if d_z == 0 else own, x_size + (cols if d_z == 0 else 0)), bf16)
                for d_y in range(n_y)
                for d_z in range(n_z)
            ],
            [SMEM] + [VMEM] * (n_a + 2 + len(projs)),
            scratch=scratch
            + [pltpu.VMEM((x_size, x_size), f32), pltpu.VMEM((z_cells, y_cells, group * rank), bf16)],
            name="gram",
        )(flags, x_factor.T, *chunks[-1], gram, *projs)
        received = [pieces[0]]
        for d_y in range(n_y):
            for d_z in range(n_z):
                if d_y or d_z:
                    pairs = [
                        (y * n_z + z, (y + d_y) % n_y * n_z + (z + d_z) % n_z)
                        for y in range(n_y)
                        for z in range(n_z)
                    ]
                    received.append(lax.ppermute(pieces[d_y * n_z + d_z], ("gy", "gz"), pairs))
    else:
        proj = jnp.concatenate(projs, axis=1)
        full = lax.all_to_all(
            proj.reshape(n_y, layers, y_cells, group * rank), "gy", split_axis=0, concat_axis=0, tiled=True
        )
        blocks = lax.all_to_all(
            gram.astype(bf16).reshape(owners, own, x_size), ("gy", "gz"), split_axis=0, concat_axis=0, tiled=True
        )
        full = full.transpose(0, 2, 1, 3).reshape(n_y, y_cells, cols)
        received = []
        for d_y in range(n_y):
            for d_z in range(n_z):
                source = (g_y - d_y + n_y) % n_y * n_z + (g_z - d_z + n_z) % n_z
                block = lax.dynamic_index_in_dim(blocks, source, 0, keepdims=False)
                if d_z == 0:
                    block = jnp.pad(block, ((0, piece_rows - own), (0, 0)))
                    side = lax.dynamic_index_in_dim(full, (g_y - d_y + n_y) % n_y, 0, keepdims=False)
                    side = jnp.pad(side, ((0, piece_rows - y_cells), (0, 0)))
                    block = jnp.concatenate([block, side], axis=1)
                received.append(block)
    payload = call(
        functools.partial(
            layer_kernel, n_y, n_z, own, layers, 1.0 / (variables * rank), 1.0 / (variables * rows * owners)
        ),
        [sds((max(own, y_rank), x_size + layers * y_size), bf16)],
        [SMEM] + [VMEM] * (1 + owners),
        scratch=[pltpu.VMEM((layers, y_size, group * rank), bf16)],
        name="layer",
    )(flags, y_factor.T, *received)[0]
    payloads = [payload] + [lax.ppermute(payload, "ga", ring_pairs(n_a, k)) for k in range(1, n_a)]
    x_gram, products = call(
        functools.partial(last_kernel, x_size, n_a),
        [sds((own, x_size), f32), sds((layers, y_rank, y_size), f32)],
        [VMEM] * n_a,
        name="last",
        limit=8,
    )(*payloads)
    return (
        new_fields.reshape(fields.shape),
        x_gram,
        jnp.swapaxes(products, 1, 2),
    )


def solution(mesh):
    block = P(None, "gy", "gz", "ga")
    in_specs = (block, block, block, P(), P(), P(), P())
    out_specs = (block, P(("gy", "gz"), None), P(("gz", "gy"), None, None))
    return jax.shard_map(shards, mesh=mesh, in_specs=in_specs, out_specs=out_specs, check_vma=False)
```

```python
import functools

import jax
import jax.numpy as jnp
from jax import lax
from jax.experimental import pallas as pl
from jax.experimental.pallas import tpu as pltpu
from jax.sharding import PartitionSpec as P


time_step = 0.4
old_share, new_share = 0.75, 0.25
TILE = 32
SUB = 16
VMEM = pl.BlockSpec(memory_space=pltpu.VMEM)
SMEM = pl.BlockSpec(memory_space=pltpu.SMEM)
ANY = pl.BlockSpec(memory_space=pl.ANY)
f32, bf16 = jnp.float32, jnp.bfloat16
sds = jax.ShapeDtypeStruct
MIB = 1024 * 1024


def swap_pairs(count, turn):
    if turn == 0:
        return [(i, i ^ 1) for i in range(count)]
    return [(i, (i + (1 if i % 2 else -1)) % count) for i in range(count)]


def turns(count):
    return 1 if count == 2 else 2


def ring_pairs(count, step):
    return [(i, (i + step) % count) for i in range(count)]


def corner_mask(lanes):
    row = lax.broadcasted_iota(jnp.int32, (8, lanes), 0)
    lane = lax.broadcasted_iota(jnp.int32, (8, lanes), 1)
    return jnp.where(
        ((row == 0) & (lane == 0)) | ((row == 1) & (lane == lanes - 1)), 1.0, 0.0
    ).astype(bf16)


def rows_of(ref, v, segments):
    return jnp.concatenate([ref[v, first : first + count, :] for first, count in segments], axis=0)


def pack_kernel(z_cells, counts, plan, f_hbm, *refs):
    outs, (f_ref, sem) = refs[:-2], refs[-2:]
    variables, rows, lanes = f_ref.shape
    n_y, n_z, n_a = counts
    n_sem = sem.shape[0]
    step = variables // n_sem
    loads = [
        pltpu.make_async_copy(
            f_hbm.at[pl.ds(i * step, step)], f_ref.at[pl.ds(i * step, step)], sem.at[i]
        )
        for i in range(n_sem)
    ]
    for load in loads:
        load.start()
    y_refs, outs = outs[: turns(n_y)], outs[turns(n_y) :]
    x_refs, z_refs = outs[: turns(n_a)], outs[turns(n_a) :]
    odd_y, odd_z, odd_a = (lax.rem(lax.axis_index(a), 2) for a in ("gy", "gz", "ga"))
    pick = corner_mask(lanes)
    for v in range(variables):
        if v % step == 0:
            loads[v // step].wait()
        for c, segments in enumerate(plan):
            size = sum(count for _, count in segments)
            at = 0
            for first, count in segments:
                y_count = count // z_cells
                for turn in range(turns(n_z)):
                    start = first + jnp.where(odd_z == turn, z_cells - 1, 0)
                    z_refs[c * turns(n_z) + turn][v, at : at + y_count, :] = f_ref[
                        v, pl.ds(start, y_count, stride=z_cells), :
                    ].astype(bf16)
                at += y_count
            edges = lax.dot_general(
                pick, rows_of(f_ref, v, segments).astype(bf16), (((1,), (1,)), ((), ())),
                preferred_element_type=f32,
            )
            for turn in range(turns(n_a)):
                x_refs[turn][c : c + 1, v * size : (v + 1) * size] = jnp.where(
                    odd_a == turn, edges[1:2, :], edges[0:1, :]
                )
        for turn in range(turns(n_y)):
            y_refs[turn][v] = jnp.where(
                odd_y == turn, f_ref[v, rows - z_cells :, :], f_ref[v, :z_cells, :]
            )


def low_high(axis, count, halos):
    index = lax.axis_index(axis)
    odd = lax.rem(index, 2)
    a, b = halos[0], halos[-1]

    def pick(value_of):
        first, second = value_of(a), value_of(b)
        low = jnp.where(odd == 1, first, second)
        high = jnp.where(odd == 1, second, first)
        zero = jnp.zeros_like(low)
        return jnp.where(index > 0, low, zero), jnp.where(index < count - 1, high, zero)

    return pick


def mix_kernel(r_ref, after, out_ref):
    count = r_ref.shape[0]
    size = out_ref.shape[0]
    spread = jnp.where(
        lax.broadcasted_iota(jnp.int32, (size, count), 0) // SUB
        == lax.broadcasted_iota(jnp.int32, (size, count), 1),
        1.0,
        0.0,
    ).astype(bf16)
    scaled = (r_ref[...] * (new_share * time_step)).astype(bf16)
    left = lax.dot_general(spread, scaled, (((1,), (0,)), ((), ())), preferred_element_type=f32)
    both = lax.dot_general(
        left.astype(bf16), spread, (((1,), (1,)), ((), ())), preferred_element_type=f32
    )
    row = lax.broadcasted_iota(jnp.int32, (size, size), 0)
    col = lax.broadcasted_iota(jnp.int32, (size, size), 1)
    out_ref[...] = jnp.where(row % SUB == col % SUB, both, 0.0).astype(bf16)


def stencil_kernel(
    z_cells, counts, index, segments, has_prior, has_y, diffusion, f_hbm, s_hbm, vel_hbm, mix_ref, *rest
):
    n_y, n_z, parts = counts
    x_refs, rest = rest[: turns(parts)], rest[turns(parts) :]
    z_refs, rest = rest[: turns(n_z)], rest[turns(n_z) :]
    if has_y:
        y_refs, rest = rest[: turns(n_y)], rest[turns(n_y) :]
    rest = rest[1:] if has_prior else rest
    new_hbm, rest = rest[0], rest[1:]
    snaps, (padded, edge, zface, react, start_ref, vel_ref, new_ref, f_sem, in_sem, vel_sem, out_sem) = (
        rest[:parts], rest[parts:]
    )
    variables, rows, lanes = f_hbm.shape
    pad = -(-z_cells // 8) * 8
    span = segments[0][1] + 2 * pad
    tile = TILE
    chunk = sum(count for _, count in segments)
    me = lax.axis_index("ga")
    is_buffer = me == parts - 1

    loads, starts, winds = [], [], []
    for i, (first, count) in enumerate(segments):
        low, high = max(first - pad, 0), min(first + count + pad, rows)
        loads.append(
            pltpu.make_async_copy(
                f_hbm.at[:, pl.ds(low, high - low), :],
                padded.at[:, pl.ds(i * span + low - first + pad, high - low), :],
                f_sem.at[i],
            )
        )
        loads[-1].start()
    tile_rows = [first + k * tile for first, count in segments for k in range(count // tile)]
    for t, row in enumerate(tile_rows):
        source, target = pl.ds(row, tile), pl.ds(t * tile, tile)
        starts.append(
            pltpu.make_async_copy(s_hbm.at[:, source, :], start_ref.at[:, target, :], in_sem.at[t])
        )
        winds.append(
            pltpu.make_async_copy(vel_hbm.at[:, source, :], vel_ref.at[:, target, :], vel_sem.at[t])
        )
        starts[-1].start()
        winds[-1].start()

    put = corner_mask(lanes)
    side = lax.broadcasted_iota(jnp.int32, (8, chunk), 0)
    y_count = chunk // z_cells
    x_pair = low_high("ga", parts, x_refs)
    z_pair = low_high("gz", n_z, z_refs)
    for v in range(variables):
        first, second = x_pair(lambda ref: ref[index : index + 1, v * chunk : (v + 1) * chunk])
        first = jnp.broadcast_to(first, (8, chunk))
        second = jnp.broadcast_to(second, (8, chunk))
        both = jnp.where(side == 0, first, jnp.where(side == 1, second, 0.0)).astype(bf16)
        edge[v] = lax.dot_general(both, put, (((0,), (0,)), ((), ())), preferred_element_type=f32)
        first, second = z_pair(lambda ref: ref[v].astype(f32))
        zface[v, pl.ds(0, y_count, stride=z_cells), :] = first
        zface[v, pl.ds(z_cells - 1, y_count, stride=z_cells), :] = second
    for load in loads:
        load.wait()
    for i, (first, count) in enumerate(segments):
        if first == 0 or first + count == rows:
            low, high = low_high("gy", n_y, y_refs)(lambda ref: ref[...])
            if first == 0:
                padded[:, i * span + pad - z_cells : i * span + pad, :] = low
            else:
                padded[:, i * span + pad + count : i * span + pad + count + z_cells, :] = high

    rate = new_share * time_step
    group = variables // parts
    tiles = segments[0][1] // tile

    def out_copy(t):
        row = segments[0][0] + t * tile
        if len(segments) > 1:
            gap = segments[1][0] - segments[0][0] - segments[0][1]
            row = row + lax.div(t, tiles) * gap
        at = pl.multiple_of(t * tile, tile)
        return pltpu.make_async_copy(
            new_ref.at[:, pl.ds(at, tile), :],
            new_hbm.at[:, pl.ds(pl.multiple_of(row, 8), tile), :],
            out_sem.at[t],
        )

    def in_copies(t):
        row = segments[0][0] + t * tile
        if len(segments) > 1:
            gap = segments[1][0] - segments[0][0] - segments[0][1]
            row = row + lax.div(t, tiles) * gap
        source, target = pl.ds(pl.multiple_of(row, 8), tile), pl.ds(pl.multiple_of(t * tile, tile), tile)
        return (
            pltpu.make_async_copy(s_hbm.at[:, source, :], start_ref.at[:, target, :], in_sem.at[t]),
            pltpu.make_async_copy(vel_hbm.at[:, source, :], vel_ref.at[:, target, :], vel_sem.at[t]),
        )

    def body(t, carry):
        at = pl.multiple_of(t * tile, tile)
        base = pl.multiple_of(at + lax.div(t, tiles) * (2 * pad), 8)
        blocks = []
        for sub in range(tile // SUB):
            blocks.append(
                jnp.concatenate(
                    [padded[w, pl.ds(base + pad + sub * SUB, SUB), :].astype(bf16) for w in range(variables)],
                    axis=0,
                )
            )
        react[...] = jnp.dot(
            mix_ref[...], jnp.concatenate(blocks, axis=1), preferred_element_type=f32
        )
        for copy in in_copies(t):
            copy.wait()
        lane = lax.broadcasted_iota(jnp.int32, (tile, lanes), 1)
        z_at = lax.rem(lax.broadcasted_iota(jnp.int32, (tile, lanes), 0), z_cells)
        v_x = vel_ref[0, pl.ds(at, tile), :] * (0.5 * rate)
        v_y = vel_ref[1, pl.ds(at, tile), :] * (0.5 * rate)
        v_z = vel_ref[2, pl.ds(at, tile), :] * (0.5 * rate)
        for part in range(parts):
            target = lax.rem(me + part, parts)
            for j in range(group):
                v = target * group + j
                spread = diffusion[v] * rate
                center = padded[v, pl.ds(base + pad, tile), :]
                y_minus = padded[v, pl.ds(base + pad - z_cells, tile), :]
                y_plus = padded[v, pl.ds(base + pad + z_cells, tile), :]
                face = zface[v, pl.ds(at, tile), :]
                z_minus = jnp.where(z_at == 0, face, padded[v, pl.ds(base + pad - 1, tile), :])
                z_plus = jnp.where(z_at == z_cells - 1, face, padded[v, pl.ds(base + pad + 1, tile), :])
                sides = edge[v, pl.ds(at, tile), :]
                x_minus = jnp.where(lane == 0, sides, pltpu.roll(center, 1, 1))
                x_plus = jnp.where(lane == lanes - 1, sides, pltpu.roll(center, lanes - 1, 1))
                mixed = jnp.concatenate(
                    [
                        react[pl.ds(pl.multiple_of(v * SUB, SUB), SUB), sub * lanes : (sub + 1) * lanes]
                        for sub in range(tile // SUB)
                    ],
                    axis=0,
                )
                around = (y_plus + y_minus) + (z_plus + z_minus) + (x_plus + x_minus)
                carried = v_x * (x_plus - x_minus) + v_y * (y_plus - y_minus) + v_z * (z_plus - z_minus)
                value = (
                    old_share * start_ref[v, pl.ds(at, tile), :]
                    + (new_share - 6.0 * spread) * center
                    + (spread * around - carried)
                    + mixed
                )
                value = jnp.where(is_buffer, center, value)
                new_ref[v, pl.ds(at, tile), :] = value
                snaps[part][j, pl.ds(at, tile), :] = value.astype(bf16)
        out_copy(t).start()
        return carry

    lax.fori_loop(0, chunk // tile, body, 0)
    for t in range(chunk // tile):
        out_copy(t).wait()


def gather_rows(parts, me, pieces, wide):
    group, rows, lanes = pieces[0].shape
    for part in range(parts):
        source = lax.rem(me - part + parts, parts)
        at = pl.multiple_of(source * lanes, lanes)
        for j in range(group):
            wide[j * rows : (j + 1) * rows, pl.ds(at, lanes)] = pieces[part][j]


def project(z_cells, group, rows, xf_ref, wide, proj, store):
    y_cells = rows // z_cells
    proj[...] = lax.dot_general(
        wide[...], xf_ref[...], (((1,), (1,)), ((), ())), preferred_element_type=f32
    )
    for z in range(z_cells):
        cols = [proj[pl.ds(j * rows + z, y_cells, stride=z_cells), :] for j in range(group)]
        store(z, jnp.concatenate(cols, axis=1).astype(bf16))


def part_gram_kernel(z_cells, parts, has_prior, xf_ref, *refs):
    pieces, refs = refs[:parts], refs[parts:]
    if has_prior:
        prior, refs = refs[0], refs[1:]
    gram_ref, proj_ref, wide, proj = refs
    group, rows, _ = pieces[0].shape
    gather_rows(parts, lax.axis_index("ga"), pieces, wide)
    data = wide[...]
    gram = lax.dot_general(data, data, (((0,), (0,)), ((), ())), preferred_element_type=f32)
    gram_ref[...] = prior[...] + gram if has_prior else gram

    def store(z, value):
        proj_ref[z] = value

    project(z_cells, group, rows, xf_ref, wide, proj, store)


def last_gram_kernel(z_cells, parts, n_y, n_z, plan, xf_ref, *refs):
    priors = len(plan) - 1
    pieces, refs = refs[:parts], refs[parts:]
    prior, refs = refs[0], refs[1:]
    prior_proj, refs = refs[:priors], refs[priors:]
    outs, (wide, proj, gram, full) = refs[: n_y * n_z], refs[n_y * n_z :]
    group, rows, _ = pieces[0].shape
    me, my_y, my_z = (lax.axis_index(a) for a in ("ga", "gy", "gz"))
    gather_rows(parts, me, pieces, wide)

    def place(z, value, segments):
        at = 0
        for first, count in segments:
            y_count = count // z_cells
            full[z, first // z_cells : first // z_cells + y_count, :] = value[at : at + y_count]
            at += y_count

    project(z_cells, group, rows, xf_ref, wide, proj, lambda z, value: place(z, value, plan[-1]))
    for i in range(priors):
        for z in range(z_cells):
            place(z, prior_proj[i][z], plan[i])
    data = wide[...]
    gram[...] = prior[...] + lax.dot_general(
        data, data, (((0,), (0,)), ((), ())), preferred_element_type=f32
    )
    own = gram.shape[0] // (n_y * n_z)
    width = gram.shape[1]
    layers = z_cells // n_y
    cols = full.shape[2]
    for d_y in range(n_y):
        for d_z in range(n_z):
            out = outs[d_y * n_z + d_z]
            y_to, z_to = lax.rem(my_y + d_y, n_y), lax.rem(my_z + d_z, n_z)
            at = pl.multiple_of((y_to * n_z + z_to) * own, own)
            out[:own, :width] = gram[pl.ds(at, own), :].astype(bf16)
            if d_z == 0:
                for layer in range(layers):
                    out[: full.shape[1], width + layer * cols : width + (layer + 1) * cols] = full[
                        y_to * layers + layer
                    ]


def layer_kernel(n_y, n_z, own, layers, y_scale, x_scale, yf_ref, *refs):
    pieces, (out_ref, m_ref) = refs[: n_y * n_z], refs[n_y * n_z :]
    rank, y_size = yf_ref.shape
    y_cells = y_size // n_y
    cols = m_ref.shape[2]
    width = pieces[0].shape[1] - layers * cols
    my_y = lax.axis_index("gy")
    for d_y in range(n_y):
        source = lax.rem(my_y - d_y + n_y, n_y)
        at = pl.multiple_of(source * y_cells, y_cells)
        for layer in range(layers):
            m_ref[layer, pl.ds(at, y_cells), :] = pieces[d_y * n_z][
                :y_cells, width + layer * cols : width + (layer + 1) * cols
            ]
    for layer in range(layers):
        m = m_ref[layer]
        y_gram = lax.dot_general(m, m, (((1,), (1,)), ((), ())), preferred_element_type=f32) * y_scale
        prod = lax.dot_general(
            yf_ref[...], y_gram, (((1,), (0,)), ((), ())), preferred_element_type=f32,
            precision=lax.Precision.HIGHEST,
        )
        if own != rank:
            out_ref[...] = jnp.zeros_like(out_ref)
        out_ref[:rank, width + layer * y_size : width + (layer + 1) * y_size] = prod.astype(bf16)
    total = pieces[0][:own, :width].astype(f32)
    for i in range(1, n_y * n_z):
        total = total + pieces[i][:own, :width].astype(f32)
    out_ref[:own, :width] = (total * x_scale).astype(bf16)


def last_kernel(width, parts, *refs):
    pieces, (gram_ref, prod_ref) = refs[:parts], refs[parts:]
    total = pieces[0][...].astype(f32)
    for i in range(1, parts):
        total = total + pieces[i][...].astype(f32)
    gram_ref[...] = total[: gram_ref.shape[0], :width]
    layers, rank, y_size = prod_ref.shape
    for layer in range(layers):
        prod_ref[layer] = total[:rank, width + layer * y_size : width + (layer + 1) * y_size]


def call(kernel, out_shapes, in_specs, scratch=(), limit=16, flops=0, moved=0):
    return pl.pallas_call(
        kernel,
        out_shape=out_shapes,
        in_specs=in_specs,
        out_specs=[VMEM] * len(out_shapes),
        scratch_shapes=list(scratch),
        cost_estimate=pl.CostEstimate(flops=flops, bytes_accessed=moved, transcendentals=0),
        compiler_params=pltpu.CompilerParams(vmem_limit_bytes=limit * MIB),
    )


def shards(fields, section_start, velocity, diffusivity, reaction, x_factor, y_factor):
    variables, y_cells, z_cells, lanes = fields.shape
    rows = y_cells * z_cells
    n_y, n_z, n_a = (lax.axis_size(a) for a in ("gy", "gz", "ga"))
    g_y, g_z, _ = (lax.axis_index(a) for a in ("gy", "gz", "ga"))
    f = fields.reshape(variables, rows, lanes)
    s = section_start.reshape(variables, rows, lanes)
    vel = velocity.reshape(3, rows, lanes)
    x_size = n_a * lanes
    y_size = n_y * y_cells
    rank, y_rank = x_factor.shape[1], y_factor.shape[1]
    group = variables // n_a
    owners = n_y * n_z
    own = x_size // owners
    layers = z_cells // n_y
    pad = -(-z_cells // 8) * 8
    tile = TILE
    quarter = rows // 4
    plan = (((quarter, 2 * quarter),), ((0, quarter), (3 * quarter, quarter)))
    chunk = 2 * quarter
    y_part = chunk // z_cells
    counts = (n_y, n_z, n_a)
    in_hbm = functools.partial(pltpu.with_memory_space_constraint, memory_space=pltpu.HBM)
    packed = call(
        functools.partial(pack_kernel, z_cells, counts, plan),
        [sds((variables, z_cells, lanes), f32)] * turns(n_y)
        + [sds((len(plan), variables * chunk), f32)] * turns(n_a)
        + [sds((variables, y_part, lanes), bf16)] * (turns(n_z) * len(plan)),
        [ANY],
        scratch=[
            pltpu.VMEM((variables, rows, lanes), f32),
            pltpu.SemaphoreType.DMA((min(variables, 8),)),
        ],
        limit=12,
    )(in_hbm(f))
    y_faces, packed = packed[: turns(n_y)], packed[turns(n_y) :]
    x_edges, z_faces = packed[: turns(n_a)], packed[turns(n_a) :]

    def halo(axis, count, faces):
        return [lax.ppermute(face, axis, swap_pairs(count, turn)) for turn, face in enumerate(faces)]

    mix = call(
        mix_kernel, [sds((variables * SUB, variables * SUB), bf16)], [VMEM, ANY], limit=8
    )(reaction, y_faces[0])[0]

    def stencil(index, prior, x_halos, z_halos, y_halos):
        segments = plan[index]
        tiles = chunk // tile
        operands = [diffusivity, f, in_hbm(s), in_hbm(vel), mix, *x_halos, *z_halos, *y_halos]
        specs = [SMEM, ANY, ANY, ANY] + [VMEM] * (len(operands) - 4)
        aliases = {}
        if prior is not None:
            aliases = {len(operands): 0}
            operands.append(prior)
            specs.append(ANY)
        return pl.pallas_call(
            functools.partial(stencil_kernel, z_cells, counts, index, segments, prior is not None, bool(y_halos)),
            out_shape=[sds((variables, rows, lanes), f32)] + [sds((group, chunk, lanes), bf16)] * n_a,
            in_specs=specs,
            out_specs=[ANY] + [VMEM] * n_a,
            scratch_shapes=[
                pltpu.VMEM((variables, chunk + 2 * pad * len(segments), lanes), f32),
                pltpu.VMEM((variables, chunk, lanes), f32),
                pltpu.VMEM((variables, chunk, lanes), f32),
                pltpu.VMEM((variables * SUB, tile // SUB * lanes), f32),
                pltpu.VMEM((variables, chunk, lanes), f32),
                pltpu.VMEM((3, chunk, lanes), f32),
                pltpu.VMEM((variables, chunk, lanes), f32),
                pltpu.SemaphoreType.DMA((len(segments),)),
                pltpu.SemaphoreType.DMA((tiles,)),
                pltpu.SemaphoreType.DMA((tiles,)),
                pltpu.SemaphoreType.DMA((tiles,)),
            ],
            input_output_aliases=aliases,
            name="stencil",
            compiler_params=pltpu.CompilerParams(vmem_limit_bytes=20 * MIB),
        )(*operands)

    def exchange(snaps):
        received = [snaps[0]]
        for k in range(1, n_a):
            received.append(lax.ppermute(snaps[k], "ga", ring_pairs(n_a, k)))
        return received

    early_z, late_z = z_faces[: turns(n_z)], z_faces[turns(n_z) :]
    z_halos = halo("gz", n_z, early_z)
    x_halos = halo("ga", n_a, x_edges)
    results = stencil(0, None, x_halos, z_halos, ())
    new_fields = results[0]
    chunks = [exchange(results[1:])]
    y_faces, late_z, _ = lax.optimization_barrier((tuple(y_faces), tuple(late_z), results[2]))
    y_halos = halo("gy", n_y, y_faces)
    z_halos = halo("gz", n_z, late_z)
    results = stencil(1, new_fields, x_halos, z_halos, y_halos)
    new_fields = results[0]
    chunks.append(exchange(results[1:]))

    scratch = [pltpu.VMEM((group * chunk, x_size), bf16), pltpu.VMEM((group * chunk, rank), f32)]
    gram, projs = None, []
    direct = owners <= 8
    for index in range(len(plan) - 1 if direct else len(plan)):
        gram, proj = call(
            functools.partial(part_gram_kernel, z_cells, n_a, gram is not None),
            [sds((x_size, x_size), f32), sds((z_cells, y_part, group * rank), bf16)],
            [VMEM] * (n_a + 1 + (gram is not None)),
            scratch=scratch,
        )(x_factor.T, *chunks[index], *([] if gram is None else [gram]))
        projs.append(proj)
    cols = layers * group * rank
    piece_rows = max(own, y_cells)
    if direct:
        pieces = call(
            functools.partial(last_gram_kernel, z_cells, n_a, n_y, n_z, plan),
            [
                sds((piece_rows if d_z == 0 else own, x_size + (cols if d_z == 0 else 0)), bf16)
                for _ in range(n_y)
                for d_z in range(n_z)
            ],
            [VMEM] * (n_a + 2 + len(projs)),
            scratch=scratch
            + [pltpu.VMEM((x_size, x_size), f32), pltpu.VMEM((z_cells, y_cells, group * rank), bf16)],
        )(x_factor.T, *chunks[-1], gram, *projs)
        received = [pieces[0]]
        for d_y in range(n_y):
            for d_z in range(n_z):
                if d_y or d_z:
                    pairs = [
                        (y * n_z + z, (y + d_y) % n_y * n_z + (z + d_z) % n_z)
                        for y in range(n_y)
                        for z in range(n_z)
                    ]
                    received.append(lax.ppermute(pieces[d_y * n_z + d_z], ("gy", "gz"), pairs))
    else:
        half = quarter // z_cells
        proj = jnp.concatenate([projs[1][:, :half], projs[0], projs[1][:, half:]], axis=1)
        full = lax.all_to_all(
            proj.reshape(n_y, layers, y_cells, group * rank), "gy", split_axis=0, concat_axis=0, tiled=True
        )
        blocks = lax.all_to_all(
            gram.astype(bf16).reshape(owners, own, x_size), ("gy", "gz"), split_axis=0, concat_axis=0, tiled=True
        )
        full = full.transpose(0, 2, 1, 3).reshape(n_y, y_cells, cols)
        received = []
        for d_y in range(n_y):
            for d_z in range(n_z):
                source = (g_y - d_y + n_y) % n_y * n_z + (g_z - d_z + n_z) % n_z
                block = lax.dynamic_index_in_dim(blocks, source, 0, keepdims=False)
                if d_z == 0:
                    block = jnp.pad(block, ((0, piece_rows - own), (0, 0)))
                    side = lax.dynamic_index_in_dim(full, (g_y - d_y + n_y) % n_y, 0, keepdims=False)
                    side = jnp.pad(side, ((0, piece_rows - y_cells), (0, 0)))
                    block = jnp.concatenate([block, side], axis=1)
                received.append(block)
    payload = call(
        functools.partial(
            layer_kernel, n_y, n_z, own, layers, 1.0 / (variables * rank), 1.0 / (variables * rows * owners)
        ),
        [sds((max(own, y_rank), x_size + layers * y_size), bf16)],
        [VMEM] * (1 + owners),
        scratch=[pltpu.VMEM((layers, y_size, group * rank), bf16)],
    )(y_factor.T, *received)[0]
    payloads = [payload] + [lax.ppermute(payload, "ga", ring_pairs(n_a, k)) for k in range(1, n_a)]
    x_gram, products = call(
        functools.partial(last_kernel, x_size, n_a),
        [sds((own, x_size), f32), sds((layers, y_rank, y_size), f32)],
        [VMEM] * n_a,
        limit=8,
    )(*payloads)
    return (
        new_fields.reshape(fields.shape),
        x_gram,
        jnp.swapaxes(products, 1, 2),
    )


def solution(mesh):
    block = P(None, "gy", "gz", "ga")
    in_specs = (block, block, block, P(), P(), P(), P())
    out_specs = (block, P(("gy", "gz"), None), P(("gz", "gy"), None, None))

    return jax.shard_map(shards, mesh=mesh, in_specs=in_specs, out_specs=out_specs, check_vma=False)
```

```python
import functools

import jax
import jax.numpy as jnp
from jax import lax
from jax.experimental import pallas as pl
from jax.experimental.pallas import tpu as pltpu
from jax.sharding import PartitionSpec as P


time_step = 0.4
old_share, new_share = 0.75, 0.25
TILE = 32
SUB = 16
VMEM = pl.BlockSpec(memory_space=pltpu.VMEM)
SMEM = pl.BlockSpec(memory_space=pltpu.SMEM)
ANY = pl.BlockSpec(memory_space=pl.ANY)
f32, bf16 = jnp.float32, jnp.bfloat16
sds = jax.ShapeDtypeStruct
MIB = 1024 * 1024


def swap_pairs(count, turn):
    if turn == 0:
        return [(i, i ^ 1) for i in range(count)]
    return [(i, (i + (1 if i % 2 else -1)) % count) for i in range(count)]


def turns(count):
    return 1 if count == 2 else 2


def ring_pairs(count, step):
    return [(i, (i + step) % count) for i in range(count)]


def corner_mask(lanes):
    row = lax.broadcasted_iota(jnp.int32, (8, lanes), 0)
    lane = lax.broadcasted_iota(jnp.int32, (8, lanes), 1)
    return jnp.where(
        ((row == 0) & (lane == 0)) | ((row == 1) & (lane == lanes - 1)), 1.0, 0.0
    ).astype(bf16)


def rows_of(ref, v, segments):
    return jnp.concatenate([ref[v, first : first + count, :] for first, count in segments], axis=0)


def pack_kernel(z_cells, counts, plan, f_hbm, *refs):
    f_ref, outs, sem = refs[0], refs[1:-1], refs[-1]
    variables, rows, lanes = f_ref.shape
    n_y, n_z, n_a = counts
    n_sem = sem.shape[0]
    step = variables // n_sem
    loads = [
        pltpu.make_async_copy(
            f_hbm.at[pl.ds(i * step, step)], f_ref.at[pl.ds(i * step, step)], sem.at[i]
        )
        for i in range(n_sem)
    ]
    for load in loads:
        load.start()
    y_refs, outs = outs[: turns(n_y)], outs[turns(n_y) :]
    x_refs, z_refs = outs[: turns(n_a)], outs[turns(n_a) :]
    odd_y, odd_z, odd_a = (lax.rem(lax.axis_index(a), 2) for a in ("gy", "gz", "ga"))
    pick = corner_mask(lanes)
    for v in range(variables):
        if v % step == 0:
            loads[v // step].wait()
        for c, segments in enumerate(plan):
            size = sum(count for _, count in segments)
            at = 0
            for first, count in segments:
                y_count = count // z_cells
                for turn in range(turns(n_z)):
                    start = first + jnp.where(odd_z == turn, z_cells - 1, 0)
                    z_refs[c * turns(n_z) + turn][v, at : at + y_count, :] = f_ref[
                        v, pl.ds(start, y_count, stride=z_cells), :
                    ].astype(bf16)
                at += y_count
            edges = lax.dot_general(
                pick, rows_of(f_ref, v, segments).astype(bf16), (((1,), (1,)), ((), ())),
                preferred_element_type=f32,
            )
            for turn in range(turns(n_a)):
                x_refs[turn][c : c + 1, v * size : (v + 1) * size] = jnp.where(
                    odd_a == turn, edges[1:2, :], edges[0:1, :]
                )
        for turn in range(turns(n_y)):
            y_refs[turn][v] = jnp.where(
                odd_y == turn, f_ref[v, rows - z_cells :, :], f_ref[v, :z_cells, :]
            )


def low_high(axis, count, halos):
    index = lax.axis_index(axis)
    odd = lax.rem(index, 2)
    a, b = halos[0], halos[-1]

    def pick(value_of):
        first, second = value_of(a), value_of(b)
        low = jnp.where(odd == 1, first, second)
        high = jnp.where(odd == 1, second, first)
        zero = jnp.zeros_like(low)
        return jnp.where(index > 0, low, zero), jnp.where(index < count - 1, high, zero)

    return pick


def mix_kernel(r_ref, after, out_ref):
    count = r_ref.shape[0]
    size = out_ref.shape[0]
    spread = jnp.where(
        lax.broadcasted_iota(jnp.int32, (size, count), 0) // SUB
        == lax.broadcasted_iota(jnp.int32, (size, count), 1),
        1.0,
        0.0,
    ).astype(bf16)
    scaled = (r_ref[...] * (new_share * time_step)).astype(bf16)
    left = lax.dot_general(spread, scaled, (((1,), (0,)), ((), ())), preferred_element_type=f32)
    both = lax.dot_general(
        left.astype(bf16), spread, (((1,), (1,)), ((), ())), preferred_element_type=f32
    )
    row = lax.broadcasted_iota(jnp.int32, (size, size), 0)
    col = lax.broadcasted_iota(jnp.int32, (size, size), 1)
    out_ref[...] = jnp.where(row % SUB == col % SUB, both, 0.0).astype(bf16)


def stencil_kernel(
    z_cells, counts, index, segments, has_prior, has_y, diffusion, s_hbm, vel_hbm, f_ref, mix_ref, *rest
):
    n_y, n_z, parts = counts
    x_refs, rest = rest[: turns(parts)], rest[turns(parts) :]
    z_refs, rest = rest[: turns(n_z)], rest[turns(n_z) :]
    if has_y:
        y_refs, rest = rest[: turns(n_y)], rest[turns(n_y) :]
    rest = rest[1:] if has_prior else rest
    new_hbm, rest = rest[0], rest[1:]
    snaps, (ends, edge, zface, react, start_ref, vel_ref, new_ref, in_sem, vel_sem, out_sem) = (
        rest[:parts], rest[parts:]
    )
    variables, rows, lanes = f_ref.shape
    pad = -(-z_cells // 8) * 8
    tile = TILE
    chunk = sum(count for _, count in segments)
    me = lax.axis_index("ga")
    is_buffer = me == parts - 1

    starts, winds, writes = [], [], []
    tile_rows = [first + k * tile for first, count in segments for k in range(count // tile)]
    for t, row in enumerate(tile_rows):
        there, here = pl.ds(row, tile), pl.ds(t * tile, tile)
        starts.append(pltpu.make_async_copy(s_hbm.at[:, there, :], start_ref.at[:, here, :], in_sem.at[t]))
        winds.append(pltpu.make_async_copy(vel_hbm.at[:, there, :], vel_ref.at[:, here, :], vel_sem.at[t]))
        writes.append(pltpu.make_async_copy(new_ref.at[:, here, :], new_hbm.at[:, there, :], out_sem.at[t]))
        starts[-1].start()
        winds[-1].start()

    put = corner_mask(lanes)
    side = lax.broadcasted_iota(jnp.int32, (8, chunk), 0)
    y_count = chunk // z_cells
    x_pair = low_high("ga", parts, x_refs)
    z_pair = low_high("gz", n_z, z_refs)
    for v in range(variables):
        first, second = x_pair(lambda ref: ref[index : index + 1, v * chunk : (v + 1) * chunk])
        first = jnp.broadcast_to(first, (8, chunk))
        second = jnp.broadcast_to(second, (8, chunk))
        both = jnp.where(side == 0, first, jnp.where(side == 1, second, 0.0)).astype(bf16)
        edge[v] = lax.dot_general(both, put, (((0,), (0,)), ((), ())), preferred_element_type=f32)
        first, second = z_pair(lambda ref: ref[v].astype(f32))
        zface[v, pl.ds(0, y_count, stride=z_cells), :] = first
        zface[v, pl.ds(z_cells - 1, y_count, stride=z_cells), :] = second
    if has_y:
        low, high = low_high("gy", n_y, y_refs)(lambda ref: ref[...])
        ends[0, :, pad - z_cells : pad, :] = low
        ends[0, :, pad:, :] = f_ref[:, : tile + pad, :]
        ends[1, :, : tile + pad, :] = f_ref[:, rows - tile - pad :, :]
        ends[1, :, tile + pad : tile + pad + z_cells, :] = high

    rate = new_share * time_step
    group = variables // parts
    lane = lax.broadcasted_iota(jnp.int32, (SUB, lanes), 1)
    z_at = lax.rem(lax.broadcasted_iota(jnp.int32, (SUB, lanes), 0), z_cells)
    for t, row in enumerate(tile_rows):
        slot = t % 2
        blocks = []
        for sub in range(tile // SUB):
            at = row + sub * SUB
            blocks.append(
                jnp.concatenate([f_ref[w, at : at + SUB, :].astype(bf16) for w in range(variables)], axis=0)
            )
        react[slot] = jnp.dot(mix_ref[...], jnp.concatenate(blocks, axis=1), preferred_element_type=f32)
        starts[t].wait()
        winds[t].wait()
        for sub in range(tile // SUB):
            at, here = row + sub * SUB, t * tile + sub * SUB

            def rows_at(v, offset):
                if row == 0:
                    return ends[0, v, pad + sub * SUB + offset : pad + (sub + 1) * SUB + offset, :]
                if row == rows - tile:
                    return ends[1, v, pad + sub * SUB + offset : pad + (sub + 1) * SUB + offset, :]
                return f_ref[v, at + offset : at + SUB + offset, :]

            v_x = vel_ref[0, here : here + SUB, :] * (0.5 * rate)
            v_y = vel_ref[1, here : here + SUB, :] * (0.5 * rate)
            v_z = vel_ref[2, here : here + SUB, :] * (0.5 * rate)
            for part in range(parts):
                target = lax.rem(me + part, parts)
                for j in range(group):
                    v = target * group + j
                    spread = diffusion[v] * rate
                    center = rows_at(v, 0)
                    y_minus = rows_at(v, -z_cells)
                    y_plus = rows_at(v, z_cells)
                    face = zface[v, here : here + SUB, :]
                    z_minus = jnp.where(z_at == 0, face, rows_at(v, -1))
                    z_plus = jnp.where(z_at == z_cells - 1, face, rows_at(v, 1))
                    sides = edge[v, here : here + SUB, :]
                    x_minus = jnp.where(lane == 0, sides, pltpu.roll(center, 1, 1))
                    x_plus = jnp.where(lane == lanes - 1, sides, pltpu.roll(center, lanes - 1, 1))
                    mixed = react[
                        slot, pl.ds(pl.multiple_of(v * SUB, SUB), SUB), sub * lanes : (sub + 1) * lanes
                    ]
                    around = (y_plus + y_minus) + (z_plus + z_minus) + (x_plus + x_minus)
                    carried = (
                        v_x * (x_plus - x_minus) + v_y * (y_plus - y_minus) + v_z * (z_plus - z_minus)
                    )
                    value = (
                        old_share * start_ref[v, here : here + SUB, :]
                        + (new_share - 6.0 * spread) * center
                        + (spread * around - carried)
                        + mixed
                    )
                    value = jnp.where(is_buffer, center, value)
                    new_ref[v, here : here + SUB, :] = value
                    snaps[part][j, here : here + SUB, :] = value.astype(bf16)
        writes[t].start()
    for write in writes:
        write.wait()


def gather_rows(parts, me, pieces, wide):
    group, rows, lanes = pieces[0].shape
    for part in range(parts):
        source = lax.rem(me - part + parts, parts)
        at = pl.multiple_of(source * lanes, lanes)
        for j in range(group):
            wide[j * rows : (j + 1) * rows, pl.ds(at, lanes)] = pieces[part][j]


def project(z_cells, group, rows, xf_ref, wide, proj, store):
    y_cells = rows // z_cells
    proj[...] = lax.dot_general(
        wide[...], xf_ref[...], (((1,), (1,)), ((), ())), preferred_element_type=f32
    )
    for z in range(z_cells):
        cols = [proj[pl.ds(j * rows + z, y_cells, stride=z_cells), :] for j in range(group)]
        store(z, jnp.concatenate(cols, axis=1).astype(bf16))


def part_gram_kernel(z_cells, parts, has_prior, xf_ref, *refs):
    pieces, refs = refs[:parts], refs[parts:]
    if has_prior:
        prior, refs = refs[0], refs[1:]
    gram_ref, proj_ref, wide, proj = refs
    group, rows, _ = pieces[0].shape
    gather_rows(parts, lax.axis_index("ga"), pieces, wide)
    data = wide[...]
    gram = lax.dot_general(data, data, (((0,), (0,)), ((), ())), preferred_element_type=f32)
    gram_ref[...] = prior[...] + gram if has_prior else gram

    def store(z, value):
        proj_ref[z] = value

    project(z_cells, group, rows, xf_ref, wide, proj, store)


def last_gram_kernel(z_cells, parts, n_y, n_z, plan, xf_ref, *refs):
    priors = len(plan) - 1
    pieces, refs = refs[:parts], refs[parts:]
    prior, refs = refs[0], refs[1:]
    prior_proj, refs = refs[:priors], refs[priors:]
    outs, (wide, proj, gram, full) = refs[: n_y * n_z], refs[n_y * n_z :]
    group, rows, _ = pieces[0].shape
    me, my_y, my_z = (lax.axis_index(a) for a in ("ga", "gy", "gz"))
    gather_rows(parts, me, pieces, wide)

    def place(z, value, segments):
        at = 0
        for first, count in segments:
            y_count = count // z_cells
            full[z, first // z_cells : first // z_cells + y_count, :] = value[at : at + y_count]
            at += y_count

    project(z_cells, group, rows, xf_ref, wide, proj, lambda z, value: place(z, value, plan[-1]))
    for i in range(priors):
        for z in range(z_cells):
            place(z, prior_proj[i][z], plan[i])
    data = wide[...]
    gram[...] = prior[...] + lax.dot_general(
        data, data, (((0,), (0,)), ((), ())), preferred_element_type=f32
    )
    own = gram.shape[0] // (n_y * n_z)
    width = gram.shape[1]
    layers = z_cells // n_y
    cols = full.shape[2]
    for d_y in range(n_y):
        for d_z in range(n_z):
            out = outs[d_y * n_z + d_z]
            y_to, z_to = lax.rem(my_y + d_y, n_y), lax.rem(my_z + d_z, n_z)
            at = pl.multiple_of((y_to * n_z + z_to) * own, own)
            out[:own, :width] = gram[pl.ds(at, own), :].astype(bf16)
            if d_z == 0:
                for layer in range(layers):
                    out[: full.shape[1], width + layer * cols : width + (layer + 1) * cols] = full[
                        y_to * layers + layer
                    ]


def layer_kernel(n_y, n_z, own, layers, y_scale, x_scale, yf_ref, *refs):
    pieces, (out_ref, m_ref) = refs[: n_y * n_z], refs[n_y * n_z :]
    rank, y_size = yf_ref.shape
    y_cells = y_size // n_y
    cols = m_ref.shape[2]
    width = pieces[0].shape[1] - layers * cols
    my_y = lax.axis_index("gy")
    for d_y in range(n_y):
        source = lax.rem(my_y - d_y + n_y, n_y)
        at = pl.multiple_of(source * y_cells, y_cells)
        for layer in range(layers):
            m_ref[layer, pl.ds(at, y_cells), :] = pieces[d_y * n_z][
                :y_cells, width + layer * cols : width + (layer + 1) * cols
            ]
    for layer in range(layers):
        m = m_ref[layer]
        y_gram = lax.dot_general(m, m, (((1,), (1,)), ((), ())), preferred_element_type=f32) * y_scale
        prod = lax.dot_general(
            yf_ref[...], y_gram, (((1,), (0,)), ((), ())), preferred_element_type=f32,
            precision=lax.Precision.HIGHEST,
        )
        if own != rank:
            out_ref[...] = jnp.zeros_like(out_ref)
        out_ref[:rank, width + layer * y_size : width + (layer + 1) * y_size] = prod.astype(bf16)
    total = pieces[0][:own, :width].astype(f32)
    for i in range(1, n_y * n_z):
        total = total + pieces[i][:own, :width].astype(f32)
    out_ref[:own, :width] = (total * x_scale).astype(bf16)


def last_kernel(width, parts, *refs):
    pieces, (gram_ref, prod_ref) = refs[:parts], refs[parts:]
    total = pieces[0][...].astype(f32)
    for i in range(1, parts):
        total = total + pieces[i][...].astype(f32)
    gram_ref[...] = total[: gram_ref.shape[0], :width]
    layers, rank, y_size = prod_ref.shape
    for layer in range(layers):
        prod_ref[layer] = total[:rank, width + layer * y_size : width + (layer + 1) * y_size]


def call(kernel, out_shapes, in_specs, scratch=(), limit=16, flops=0, moved=0):
    return pl.pallas_call(
        kernel,
        out_shape=out_shapes,
        in_specs=in_specs,
        out_specs=[VMEM] * len(out_shapes),
        scratch_shapes=list(scratch),
        cost_estimate=pl.CostEstimate(flops=flops, bytes_accessed=moved, transcendentals=0),
        compiler_params=pltpu.CompilerParams(vmem_limit_bytes=limit * MIB),
    )


def shards(fields, section_start, velocity, diffusivity, reaction, x_factor, y_factor):
    variables, y_cells, z_cells, lanes = fields.shape
    rows = y_cells * z_cells
    n_y, n_z, n_a = (lax.axis_size(a) for a in ("gy", "gz", "ga"))
    g_y, g_z, _ = (lax.axis_index(a) for a in ("gy", "gz", "ga"))
    f = fields.reshape(variables, rows, lanes)
    s = section_start.reshape(variables, rows, lanes)
    vel = velocity.reshape(3, rows, lanes)
    x_size = n_a * lanes
    y_size = n_y * y_cells
    rank, y_rank = x_factor.shape[1], y_factor.shape[1]
    group = variables // n_a
    owners = n_y * n_z
    own = x_size // owners
    layers = z_cells // n_y
    pad = -(-z_cells // 8) * 8
    tile = TILE
    quarter = rows // 4
    plan = (((quarter, 2 * quarter),), ((0, quarter), (3 * quarter, quarter)))
    chunk = 2 * quarter
    y_part = chunk // z_cells
    counts = (n_y, n_z, n_a)
    in_hbm = functools.partial(pltpu.with_memory_space_constraint, memory_space=pltpu.HBM)
    packed = call(
        functools.partial(pack_kernel, z_cells, counts, plan),
        [sds((variables, rows, lanes), f32)]
        + [sds((variables, z_cells, lanes), f32)] * turns(n_y)
        + [sds((len(plan), variables * chunk), f32)] * turns(n_a)
        + [sds((variables, y_part, lanes), bf16)] * (turns(n_z) * len(plan)),
        [ANY],
        scratch=[pltpu.SemaphoreType.DMA((min(variables, 8),))],
        limit=12,
    )(in_hbm(f))
    f, packed = packed[0], packed[1:]
    y_faces, packed = packed[: turns(n_y)], packed[turns(n_y) :]
    x_edges, z_faces = packed[: turns(n_a)], packed[turns(n_a) :]

    def halo(axis, count, faces):
        received = []
        for turn, face in enumerate(faces):
            received.append(lax.ppermute(face, axis, swap_pairs(count, turn)))
        return received

    mix = call(
        mix_kernel, [sds((variables * SUB, variables * SUB), bf16)], [VMEM, ANY], limit=8
    )(reaction, y_faces[0])[0]

    def stencil(index, prior, x_halos, z_halos, y_halos):
        segments = plan[index]
        tiles = chunk // tile
        operands = [diffusivity, in_hbm(s), in_hbm(vel), f, mix, *x_halos, *z_halos, *y_halos]
        specs = [SMEM, ANY, ANY] + [VMEM] * (len(operands) - 3)
        aliases = {}
        if prior is not None:
            aliases = {len(operands): 0}
            operands.append(prior)
            specs.append(ANY)
        return pl.pallas_call(
            functools.partial(stencil_kernel, z_cells, counts, index, segments, prior is not None, bool(y_halos)),
            out_shape=[sds((variables, rows, lanes), f32)] + [sds((group, chunk, lanes), bf16)] * n_a,
            in_specs=specs,
            out_specs=[ANY] + [VMEM] * n_a,
            scratch_shapes=[
                pltpu.VMEM((2, variables, tile + 2 * pad, lanes), f32),
                pltpu.VMEM((variables, chunk, lanes), f32),
                pltpu.VMEM((variables, chunk, lanes), f32),
                pltpu.VMEM((2, variables * SUB, tile // SUB * lanes), f32),
                pltpu.VMEM((variables, chunk, lanes), f32),
                pltpu.VMEM((3, chunk, lanes), f32),
                pltpu.VMEM((variables, chunk, lanes), f32),
                pltpu.SemaphoreType.DMA((tiles,)),
                pltpu.SemaphoreType.DMA((tiles,)),
                pltpu.SemaphoreType.DMA((tiles,)),
            ],
            input_output_aliases=aliases,
            name="stencil",
            compiler_params=pltpu.CompilerParams(vmem_limit_bytes=20 * MIB),
        )(*operands)

    def exchange(snaps):
        received = [snaps[0]]
        for k in range(1, n_a):
            received.append(lax.ppermute(snaps[k], "ga", ring_pairs(n_a, k)))
        return received

    early_z, late_z = z_faces[: turns(n_z)], z_faces[turns(n_z) :]
    z_halos = halo("gz", n_z, early_z)
    x_halos = halo("ga", n_a, x_edges)
    y_halos = halo("gy", n_y, y_faces)
    results = stencil(0, None, x_halos, z_halos, ())
    new_fields = results[0]
    chunks = [exchange(results[1:])]
    late_z, _ = lax.optimization_barrier((tuple(late_z), results[2]))
    z_halos = halo("gz", n_z, late_z)
    results = stencil(1, new_fields, x_halos, z_halos, y_halos)
    new_fields = results[0]
    chunks.append(exchange(results[1:]))

    scratch = [pltpu.VMEM((group * chunk, x_size), bf16), pltpu.VMEM((group * chunk, rank), f32)]
    gram, projs = None, []
    direct = owners <= 8
    for index in range(len(plan) - 1 if direct else len(plan)):
        gram, proj = call(
            functools.partial(part_gram_kernel, z_cells, n_a, gram is not None),
            [sds((x_size, x_size), f32), sds((z_cells, y_part, group * rank), bf16)],
            [VMEM] * (n_a + 1 + (gram is not None)),
            scratch=scratch,
        )(x_factor.T, *chunks[index], *([] if gram is None else [gram]))
        projs.append(proj)
    cols = layers * group * rank
    piece_rows = max(own, y_cells)
    if direct:
        pieces = call(
            functools.partial(last_gram_kernel, z_cells, n_a, n_y, n_z, plan),
            [
                sds((piece_rows if d_z == 0 else own, x_size + (cols if d_z == 0 else 0)), bf16)
                for _ in range(n_y)
                for d_z in range(n_z)
            ],
            [VMEM] * (n_a + 2 + len(projs)),
            scratch=scratch
            + [pltpu.VMEM((x_size, x_size), f32), pltpu.VMEM((z_cells, y_cells, group * rank), bf16)],
        )(x_factor.T, *chunks[-1], gram, *projs)
        received = [pieces[0]]
        for d_y in range(n_y):
            for d_z in range(n_z):
                if d_y or d_z:
                    pairs = [
                        (y * n_z + z, (y + d_y) % n_y * n_z + (z + d_z) % n_z)
                        for y in range(n_y)
                        for z in range(n_z)
                    ]
                    received.append(lax.ppermute(pieces[d_y * n_z + d_z], ("gy", "gz"), pairs))
    else:
        half = quarter // z_cells
        proj = jnp.concatenate([projs[1][:, :half], projs[0], projs[1][:, half:]], axis=1)
        full = lax.all_to_all(
            proj.reshape(n_y, layers, y_cells, group * rank), "gy", split_axis=0, concat_axis=0, tiled=True
        )
        blocks = lax.all_to_all(
            gram.astype(bf16).reshape(owners, own, x_size), ("gy", "gz"), split_axis=0, concat_axis=0, tiled=True
        )
        full = full.transpose(0, 2, 1, 3).reshape(n_y, y_cells, cols)
        received = []
        for d_y in range(n_y):
            for d_z in range(n_z):
                source = (g_y - d_y + n_y) % n_y * n_z + (g_z - d_z + n_z) % n_z
                block = lax.dynamic_index_in_dim(blocks, source, 0, keepdims=False)
                if d_z == 0:
                    block = jnp.pad(block, ((0, piece_rows - own), (0, 0)))
                    side = lax.dynamic_index_in_dim(full, (g_y - d_y + n_y) % n_y, 0, keepdims=False)
                    side = jnp.pad(side, ((0, piece_rows - y_cells), (0, 0)))
                    block = jnp.concatenate([block, side], axis=1)
                received.append(block)
    payload = call(
        functools.partial(
            layer_kernel, n_y, n_z, own, layers, 1.0 / (variables * rank), 1.0 / (variables * rows * owners)
        ),
        [sds((max(own, y_rank), x_size + layers * y_size), bf16)],
        [VMEM] * (1 + owners),
        scratch=[pltpu.VMEM((layers, y_size, group * rank), bf16)],
    )(y_factor.T, *received)[0]
    payloads = [payload] + [lax.ppermute(payload, "ga", ring_pairs(n_a, k)) for k in range(1, n_a)]
    x_gram, products = call(
        functools.partial(last_kernel, x_size, n_a),
        [sds((own, x_size), f32), sds((layers, y_rank, y_size), f32)],
        [VMEM] * n_a,
        limit=8,
    )(*payloads)
    return (
        new_fields.reshape(fields.shape),
        x_gram,
        jnp.swapaxes(products, 1, 2),
    )


def solution(mesh):
    block = P(None, "gy", "gz", "ga")
    in_specs = (block, block, block, P(), P(), P(), P())
    out_specs = (block, P(("gy", "gz"), None), P(("gz", "gy"), None, None))

    return jax.shard_map(shards, mesh=mesh, in_specs=in_specs, out_specs=out_specs, check_vma=False)
```

```python
import functools

import jax
import jax.numpy as jnp
from jax import lax
from jax.experimental import pallas as pl
from jax.experimental.pallas import tpu as pltpu
from jax.sharding import PartitionSpec as P


time_step = 0.4
old_share, new_share = 0.75, 0.25
TILE = 32
SUB = 16
VMEM = pl.BlockSpec(memory_space=pltpu.VMEM)
SMEM = pl.BlockSpec(memory_space=pltpu.SMEM)
ANY = pl.BlockSpec(memory_space=pl.ANY)
f32, bf16 = jnp.float32, jnp.bfloat16
sds = jax.ShapeDtypeStruct
MIB = 1024 * 1024


def swap_pairs(count, turn):
    if turn == 0:
        return [(i, i ^ 1) for i in range(count)]
    return [(i, (i + (1 if i % 2 else -1)) % count) for i in range(count)]


def partner(count, index, step):
    if count & (count - 1) == 0:
        return index ^ step
    return (index + step) % count


def origin(count, index, step):
    if count & (count - 1) == 0:
        return index ^ step
    return (index - step + count) % count


def turns(count):
    return 1 if count == 2 else 2


def ring_pairs(count, step):
    return [(i, (i + step) % count) for i in range(count)]


def corner_mask(lanes):
    row = lax.broadcasted_iota(jnp.int32, (8, lanes), 0)
    lane = lax.broadcasted_iota(jnp.int32, (8, lanes), 1)
    return jnp.where(
        ((row == 0) & (lane == 0)) | ((row == 1) & (lane == lanes - 1)), 1.0, 0.0
    ).astype(bf16)


def rows_of(ref, v, segments):
    return jnp.concatenate([ref[v, first : first + count, :] for first, count in segments], axis=0)


def pack_kernel(z_cells, counts, plan, f_hbm, *refs):
    f_ref, outs, sem = refs[0], refs[1:-1], refs[-1]
    variables, rows, lanes = f_ref.shape
    n_y, n_z, n_a = counts
    n_sem = sem.shape[0]
    step = variables // n_sem
    loads = [
        pltpu.make_async_copy(
            f_hbm.at[pl.ds(i * step, step)], f_ref.at[pl.ds(i * step, step)], sem.at[i]
        )
        for i in range(n_sem)
    ]
    for load in loads:
        load.start()
    y_refs, outs = outs[: turns(n_y)], outs[turns(n_y) :]
    x_refs, z_refs = outs[: turns(n_a)], outs[turns(n_a) :]
    odd_y, odd_z, odd_a = (lax.rem(lax.axis_index(a), 2) for a in ("gy", "gz", "ga"))
    pick = corner_mask(lanes)
    for v in range(variables):
        if v % step == 0:
            loads[v // step].wait()
        for c, segments in enumerate(plan):
            size = sum(count for _, count in segments)
            at = 0
            for first, count in segments:
                y_count = count // z_cells
                for turn in range(turns(n_z)):
                    start = first + jnp.where(odd_z == turn, z_cells - 1, 0)
                    z_refs[c * turns(n_z) + turn][v, at : at + y_count, :] = f_ref[
                        v, pl.ds(start, y_count, stride=z_cells), :
                    ].astype(bf16)
                at += y_count
            edges = lax.dot_general(
                pick, rows_of(f_ref, v, segments).astype(bf16), (((1,), (1,)), ((), ())),
                preferred_element_type=f32,
            )
            for turn in range(turns(n_a)):
                x_refs[turn][c : c + 1, v * size : (v + 1) * size] = jnp.where(
                    odd_a == turn, edges[1:2, :], edges[0:1, :]
                )
        for turn in range(turns(n_y)):
            y_refs[turn][v] = jnp.where(
                odd_y == turn, f_ref[v, rows - z_cells :, :], f_ref[v, :z_cells, :]
            )


def low_high(axis, count, halos):
    index = lax.axis_index(axis)
    odd = lax.rem(index, 2)
    a, b = halos[0], halos[-1]

    def pick(value_of):
        first, second = value_of(a), value_of(b)
        low = jnp.where(odd == 1, first, second)
        high = jnp.where(odd == 1, second, first)
        zero = jnp.zeros_like(low)
        return jnp.where(index > 0, low, zero), jnp.where(index < count - 1, high, zero)

    return pick


def mix_kernel(r_ref, vel_hbm, after, out_ref, vel_ref, sem):
    load = pltpu.make_async_copy(vel_hbm, vel_ref, sem)
    load.start()
    count = r_ref.shape[0]
    size = out_ref.shape[0]
    spread = jnp.where(
        lax.broadcasted_iota(jnp.int32, (size, count), 0) // SUB
        == lax.broadcasted_iota(jnp.int32, (size, count), 1),
        1.0,
        0.0,
    ).astype(bf16)
    scaled = (r_ref[...] * (new_share * time_step)).astype(bf16)
    left = lax.dot_general(spread, scaled, (((1,), (0,)), ((), ())), preferred_element_type=f32)
    both = lax.dot_general(
        left.astype(bf16), spread, (((1,), (1,)), ((), ())), preferred_element_type=f32
    )
    row = lax.broadcasted_iota(jnp.int32, (size, size), 0)
    col = lax.broadcasted_iota(jnp.int32, (size, size), 1)
    out_ref[...] = jnp.where(row % SUB == col % SUB, both, 0.0).astype(bf16)
    load.wait()


def stencil_kernel(
    z_cells, counts, index, segments, has_y, diffusion, vel_ref, start_ref, f_ref, mix_ref, *rest
):
    n_y, n_z, parts = counts
    x_refs, rest = rest[: turns(parts)], rest[turns(parts) :]
    z_refs, rest = rest[: turns(n_z)], rest[turns(n_z) :]
    if has_y:
        y_refs, rest = rest[: turns(n_y)], rest[turns(n_y) :]
    new_ref, rest = rest[0], rest[1:]
    snaps, (ends, edge, zface, react) = rest[:parts], rest[parts:]
    variables, rows, lanes = f_ref.shape
    pad = -(-z_cells // 8) * 8
    tile = TILE
    chunk = sum(count for _, count in segments)
    me = lax.axis_index("ga")
    is_buffer = me == parts - 1

    tile_rows = [first + k * tile for first, count in segments for k in range(count // tile)]

    put = corner_mask(lanes)
    side = lax.broadcasted_iota(jnp.int32, (8, chunk), 0)
    y_count = chunk // z_cells
    x_pair = low_high("ga", parts, x_refs)
    z_pair = low_high("gz", n_z, z_refs)
    for v in range(variables):
        first, second = x_pair(lambda ref: ref[index : index + 1, v * chunk : (v + 1) * chunk])
        first = jnp.broadcast_to(first, (8, chunk))
        second = jnp.broadcast_to(second, (8, chunk))
        both = jnp.where(side == 0, first, jnp.where(side == 1, second, 0.0)).astype(bf16)
        edge[v] = lax.dot_general(both, put, (((0,), (0,)), ((), ())), preferred_element_type=f32)
        first, second = z_pair(lambda ref: ref[v].astype(f32))
        zface[v, pl.ds(0, y_count, stride=z_cells), :] = first
        zface[v, pl.ds(z_cells - 1, y_count, stride=z_cells), :] = second
    if has_y:
        low, high = low_high("gy", n_y, y_refs)(lambda ref: ref[...])
        ends[0, :, pad - z_cells : pad, :] = low
        ends[0, :, pad:, :] = f_ref[:, : tile + pad, :]
        ends[1, :, : tile + pad, :] = f_ref[:, rows - tile - pad :, :]
        ends[1, :, tile + pad : tile + pad + z_cells, :] = high

    rate = new_share * time_step
    group = variables // parts
    lane = lax.broadcasted_iota(jnp.int32, (SUB, lanes), 1)
    z_at = lax.rem(lax.broadcasted_iota(jnp.int32, (SUB, lanes), 0), z_cells)
    for t, row in enumerate(tile_rows):
        slot = t % 2
        blocks = []
        for sub in range(tile // SUB):
            at = row + sub * SUB
            blocks.append(
                jnp.concatenate([f_ref[w, at : at + SUB, :].astype(bf16) for w in range(variables)], axis=0)
            )
        react[slot] = jnp.dot(mix_ref[...], jnp.concatenate(blocks, axis=1), preferred_element_type=f32)
        for sub in range(tile // SUB):
            at, here = row + sub * SUB, t * tile + sub * SUB

            def rows_at(v, offset):
                if row == 0:
                    return ends[0, v, pad + sub * SUB + offset : pad + (sub + 1) * SUB + offset, :]
                if row == rows - tile:
                    return ends[1, v, pad + sub * SUB + offset : pad + (sub + 1) * SUB + offset, :]
                return f_ref[v, at + offset : at + SUB + offset, :]

            v_x = vel_ref[0, at : at + SUB, :] * (0.5 * rate)
            v_y = vel_ref[1, at : at + SUB, :] * (0.5 * rate)
            v_z = vel_ref[2, at : at + SUB, :] * (0.5 * rate)
            for part in range(parts):
                target = lax.rem(me + part, parts)
                for j in range(group):
                    v = target * group + j
                    spread = diffusion[v] * rate
                    center = rows_at(v, 0)
                    y_minus = rows_at(v, -z_cells)
                    y_plus = rows_at(v, z_cells)
                    face = zface[v, here : here + SUB, :]
                    z_minus = jnp.where(z_at == 0, face, rows_at(v, -1))
                    z_plus = jnp.where(z_at == z_cells - 1, face, rows_at(v, 1))
                    sides = edge[v, here : here + SUB, :]
                    x_minus = jnp.where(lane == 0, sides, pltpu.roll(center, 1, 1))
                    x_plus = jnp.where(lane == lanes - 1, sides, pltpu.roll(center, lanes - 1, 1))
                    mixed = react[
                        slot, pl.ds(pl.multiple_of(v * SUB, SUB), SUB), sub * lanes : (sub + 1) * lanes
                    ]
                    around = (y_plus + y_minus) + (z_plus + z_minus) + (x_plus + x_minus)
                    carried = (
                        v_x * (x_plus - x_minus) + v_y * (y_plus - y_minus) + v_z * (z_plus - z_minus)
                    )
                    value = (
                        old_share * start_ref[v, at : at + SUB, :]
                        + (new_share - 6.0 * spread) * center
                        + (spread * around - carried)
                        + mixed
                    )
                    value = jnp.where(is_buffer, center, value)
                    new_ref[v, here : here + SUB, :] = value
                    snaps[part][j, here : here + SUB, :] = value.astype(bf16)


def flush_kernel(plan, *refs):
    parts, (new_hbm, sem) = refs[: len(plan)], refs[len(plan) :]
    writes = []
    for part, segments in zip(parts, plan):
        at = 0
        for first, count in segments:
            writes.append(
                pltpu.make_async_copy(
                    part.at[:, pl.ds(at, count), :], new_hbm.at[:, pl.ds(first, count), :], sem.at[len(writes)]
                )
            )
            writes[-1].start()
            at += count
    for write in writes:
        write.wait()


def gather_rows(parts, me, pieces, wide):
    group, rows, lanes = pieces[0].shape
    for part in range(parts):
        source = lax.rem(me - part + parts, parts)
        at = pl.multiple_of(source * lanes, lanes)
        for j in range(group):
            wide[j * rows : (j + 1) * rows, pl.ds(at, lanes)] = pieces[part][j]


def project(z_cells, group, rows, xf_ref, wide, proj, store):
    y_cells = rows // z_cells
    proj[...] = lax.dot_general(
        wide[...], xf_ref[...], (((1,), (1,)), ((), ())), preferred_element_type=f32
    )
    for z in range(z_cells):
        cols = [proj[pl.ds(j * rows + z, y_cells, stride=z_cells), :] for j in range(group)]
        store(z, jnp.concatenate(cols, axis=1).astype(bf16))


def part_gram_kernel(z_cells, parts, has_prior, xf_ref, *refs):
    pieces, refs = refs[:parts], refs[parts:]
    if has_prior:
        prior, refs = refs[0], refs[1:]
    gram_ref, proj_ref, wide, proj = refs
    group, rows, _ = pieces[0].shape
    gather_rows(parts, lax.axis_index("ga"), pieces, wide)
    data = wide[...]
    gram = lax.dot_general(data, data, (((0,), (0,)), ((), ())), preferred_element_type=f32)
    gram_ref[...] = prior[...] + gram if has_prior else gram

    def store(z, value):
        proj_ref[z] = value

    project(z_cells, group, rows, xf_ref, wide, proj, store)


def last_gram_kernel(z_cells, parts, n_y, n_z, plan, xf_ref, *refs):
    priors = len(plan) - 1
    pieces, refs = refs[:parts], refs[parts:]
    prior, refs = refs[0], refs[1:]
    prior_proj, refs = refs[:priors], refs[priors:]
    outs, (wide, proj, gram, full) = refs[: n_y * n_z], refs[n_y * n_z :]
    group, rows, _ = pieces[0].shape
    me, my_y, my_z = (lax.axis_index(a) for a in ("ga", "gy", "gz"))
    gather_rows(parts, me, pieces, wide)

    def place(z, value, segments):
        at = 0
        for first, count in segments:
            y_count = count // z_cells
            full[z, first // z_cells : first // z_cells + y_count, :] = value[at : at + y_count]
            at += y_count

    project(z_cells, group, rows, xf_ref, wide, proj, lambda z, value: place(z, value, plan[-1]))
    for i in range(priors):
        for z in range(z_cells):
            place(z, prior_proj[i][z], plan[i])
    data = wide[...]
    gram[...] = prior[...] + lax.dot_general(
        data, data, (((0,), (0,)), ((), ())), preferred_element_type=f32
    )
    own = gram.shape[0] // (n_y * n_z)
    width = gram.shape[1]
    layers = z_cells // n_y
    cols = full.shape[2]
    for d_y in range(n_y):
        for d_z in range(n_z):
            out = outs[d_y * n_z + d_z]
            y_to, z_to = partner(n_y, my_y, d_y), partner(n_z, my_z, d_z)
            at = pl.multiple_of((y_to * n_z + z_to) * own, own)
            out[:own, :width] = gram[pl.ds(at, own), :].astype(bf16)
            if d_z == 0:
                for layer in range(layers):
                    out[: full.shape[1], width + layer * cols : width + (layer + 1) * cols] = full[
                        y_to * layers + layer
                    ]


def layer_kernel(n_y, n_z, own, layers, y_scale, x_scale, yf_ref, *refs):
    pieces, (out_ref, m_ref) = refs[: n_y * n_z], refs[n_y * n_z :]
    rank, y_size = yf_ref.shape
    y_cells = y_size // n_y
    cols = m_ref.shape[2]
    width = pieces[0].shape[1] - layers * cols
    my_y = lax.axis_index("gy")
    for d_y in range(n_y):
        source = origin(n_y, my_y, d_y)
        at = pl.multiple_of(source * y_cells, y_cells)
        for layer in range(layers):
            m_ref[layer, pl.ds(at, y_cells), :] = pieces[d_y * n_z][
                :y_cells, width + layer * cols : width + (layer + 1) * cols
            ]
    for layer in range(layers):
        m = m_ref[layer]
        y_gram = lax.dot_general(m, m, (((1,), (1,)), ((), ())), preferred_element_type=f32) * y_scale
        prod = lax.dot_general(
            yf_ref[...], y_gram, (((1,), (0,)), ((), ())), preferred_element_type=f32,
            precision=lax.Precision.HIGHEST,
        )
        if own != rank:
            out_ref[...] = jnp.zeros_like(out_ref)
        out_ref[:rank, width + layer * y_size : width + (layer + 1) * y_size] = prod.astype(bf16)
    total = pieces[0][:own, :width].astype(f32)
    for i in range(1, n_y * n_z):
        total = total + pieces[i][:own, :width].astype(f32)
    out_ref[:own, :width] = (total * x_scale).astype(bf16)


def last_kernel(width, parts, *refs):
    pieces, (gram_ref, prod_ref) = refs[:parts], refs[parts:]
    total = pieces[0][...].astype(f32)
    for i in range(1, parts):
        total = total + pieces[i][...].astype(f32)
    gram_ref[...] = total[: gram_ref.shape[0], :width]
    layers, rank, y_size = prod_ref.shape
    for layer in range(layers):
        prod_ref[layer] = total[:rank, width + layer * y_size : width + (layer + 1) * y_size]


def call(kernel, out_shapes, in_specs, scratch=(), limit=16, flops=0, moved=0):
    return pl.pallas_call(
        kernel,
        out_shape=out_shapes,
        in_specs=in_specs,
        out_specs=[VMEM] * len(out_shapes),
        scratch_shapes=list(scratch),
        cost_estimate=pl.CostEstimate(flops=flops, bytes_accessed=moved, transcendentals=0),
        compiler_params=pltpu.CompilerParams(vmem_limit_bytes=limit * MIB),
    )


def shards(fields, section_start, velocity, diffusivity, reaction, x_factor, y_factor):
    variables, y_cells, z_cells, lanes = fields.shape
    rows = y_cells * z_cells
    n_y, n_z, n_a = (lax.axis_size(a) for a in ("gy", "gz", "ga"))
    g_y, g_z, _ = (lax.axis_index(a) for a in ("gy", "gz", "ga"))
    f = fields.reshape(variables, rows, lanes)
    s = section_start.reshape(variables, rows, lanes)
    vel = velocity.reshape(3, rows, lanes)
    x_size = n_a * lanes
    y_size = n_y * y_cells
    rank, y_rank = x_factor.shape[1], y_factor.shape[1]
    group = variables // n_a
    owners = n_y * n_z
    own = x_size // owners
    layers = z_cells // n_y
    pad = -(-z_cells // 8) * 8
    tile = TILE
    quarter = rows // 4
    plan = (((quarter, 2 * quarter),), ((0, quarter), (3 * quarter, quarter)))
    chunk = 2 * quarter
    y_part = chunk // z_cells
    counts = (n_y, n_z, n_a)
    in_hbm = functools.partial(pltpu.with_memory_space_constraint, memory_space=pltpu.HBM)
    packed = call(
        functools.partial(pack_kernel, z_cells, counts, plan),
        [sds((variables, rows, lanes), f32)]
        + [sds((variables, z_cells, lanes), f32)] * turns(n_y)
        + [sds((len(plan), variables * chunk), f32)] * turns(n_a)
        + [sds((variables, y_part, lanes), bf16)] * (turns(n_z) * len(plan)),
        [ANY],
        scratch=[pltpu.SemaphoreType.DMA((min(variables, 8),))],
        limit=12,
    )(in_hbm(f))
    f, packed = packed[0], packed[1:]
    y_faces, packed = packed[: turns(n_y)], packed[turns(n_y) :]
    x_edges, z_faces = packed[: turns(n_a)], packed[turns(n_a) :]

    def halo(axis, count, faces):
        received = []
        for turn, face in enumerate(faces):
            received.append(lax.ppermute(face, axis, swap_pairs(count, turn)))
        return received

    mix, vel = call(
        mix_kernel,
        [sds((variables * SUB, variables * SUB), bf16), sds(vel.shape, f32)],
        [VMEM, ANY, ANY],
        scratch=[pltpu.SemaphoreType.DMA],
        limit=8,
    )(reaction, in_hbm(vel), y_faces[0])

    def stencil(index, x_halos, z_halos, y_halos):
        segments = plan[index]
        operands = [diffusivity, vel, s, f, mix, *x_halos, *z_halos, *y_halos]
        return pl.pallas_call(
            functools.partial(stencil_kernel, z_cells, counts, index, segments, bool(y_halos)),
            out_shape=[sds((variables, chunk, lanes), f32)] + [sds((group, chunk, lanes), bf16)] * n_a,
            in_specs=[SMEM] + [VMEM] * (len(operands) - 1),
            out_specs=[VMEM] * (n_a + 1),
            scratch_shapes=[
                pltpu.VMEM((2, variables, tile + 2 * pad, lanes), f32),
                pltpu.VMEM((variables, chunk, lanes), f32),
                pltpu.VMEM((variables, chunk, lanes), f32),
                pltpu.VMEM((2, variables * SUB, tile // SUB * lanes), f32),
            ],
            name="stencil",
            compiler_params=pltpu.CompilerParams(vmem_limit_bytes=20 * MIB),
        )(*operands)

    def exchange(snaps):
        received = [snaps[0]]
        for k in range(1, n_a):
            received.append(lax.ppermute(snaps[k], "ga", ring_pairs(n_a, k)))
        return received

    early_z, late_z = z_faces[: turns(n_z)], z_faces[turns(n_z) :]
    z_halos = halo("gz", n_z, early_z)
    x_halos = halo("ga", n_a, x_edges)
    y_halos = halo("gy", n_y, y_faces)
    results = stencil(0, x_halos, z_halos, ())
    news = [results[0]]
    chunks = [exchange(results[1:])]
    late_z, _ = lax.optimization_barrier((tuple(late_z), results[2]))
    z_halos = halo("gz", n_z, late_z)
    results = stencil(1, x_halos, z_halos, y_halos)
    news.append(results[0])
    chunks.append(exchange(results[1:]))
    new_fields = pl.pallas_call(
        functools.partial(flush_kernel, plan),
        out_shape=sds((variables, rows, lanes), f32),
        in_specs=[VMEM] * len(plan),
        out_specs=ANY,
        scratch_shapes=[pltpu.SemaphoreType.DMA((sum(len(segments) for segments in plan),))],
        name="flush",
        compiler_params=pltpu.CompilerParams(vmem_limit_bytes=4 * MIB),
    )(*news)

    scratch = [pltpu.VMEM((group * chunk, x_size), bf16), pltpu.VMEM((group * chunk, rank), f32)]
    gram, projs = None, []
    direct = owners <= 8
    for index in range(len(plan) - 1 if direct else len(plan)):
        gram, proj = call(
            functools.partial(part_gram_kernel, z_cells, n_a, gram is not None),
            [sds((x_size, x_size), f32), sds((z_cells, y_part, group * rank), bf16)],
            [VMEM] * (n_a + 1 + (gram is not None)),
            scratch=scratch,
        )(x_factor.T, *chunks[index], *([] if gram is None else [gram]))
        projs.append(proj)
    cols = layers * group * rank
    piece_rows = max(own, y_cells)
    if direct:
        pieces = call(
            functools.partial(last_gram_kernel, z_cells, n_a, n_y, n_z, plan),
            [
                sds((piece_rows if d_z == 0 else own, x_size + (cols if d_z == 0 else 0)), bf16)
                for _ in range(n_y)
                for d_z in range(n_z)
            ],
            [VMEM] * (n_a + 2 + len(projs)),
            scratch=scratch
            + [pltpu.VMEM((x_size, x_size), f32), pltpu.VMEM((z_cells, y_cells, group * rank), bf16)],
        )(x_factor.T, *chunks[-1], gram, *projs)
        received = [pieces[0]]
        for d_y in range(n_y):
            for d_z in range(n_z):
                if d_y or d_z:
                    pairs = [
                        (y * n_z + z, partner(n_y, y, d_y) * n_z + partner(n_z, z, d_z))
                        for y in range(n_y)
                        for z in range(n_z)
                    ]
                    received.append(lax.ppermute(pieces[d_y * n_z + d_z], ("gy", "gz"), pairs))
    else:
        half = quarter // z_cells
        proj = jnp.concatenate([projs[1][:, :half], projs[0], projs[1][:, half:]], axis=1)
        full = lax.all_to_all(
            proj.reshape(n_y, layers, y_cells, group * rank), "gy", split_axis=0, concat_axis=0, tiled=True
        )
        blocks = lax.all_to_all(
            gram.astype(bf16).reshape(owners, own, x_size), ("gy", "gz"), split_axis=0, concat_axis=0, tiled=True
        )
        full = full.transpose(0, 2, 1, 3).reshape(n_y, y_cells, cols)
        received = []
        for d_y in range(n_y):
            for d_z in range(n_z):
                source = origin(n_y, g_y, d_y) * n_z + origin(n_z, g_z, d_z)
                block = lax.dynamic_index_in_dim(blocks, source, 0, keepdims=False)
                if d_z == 0:
                    block = jnp.pad(block, ((0, piece_rows - own), (0, 0)))
                    side = lax.dynamic_index_in_dim(full, origin(n_y, g_y, d_y), 0, keepdims=False)
                    side = jnp.pad(side, ((0, piece_rows - y_cells), (0, 0)))
                    block = jnp.concatenate([block, side], axis=1)
                received.append(block)
    payload = call(
        functools.partial(
            layer_kernel, n_y, n_z, own, layers, 1.0 / (variables * rank), 1.0 / (variables * rows * owners)
        ),
        [sds((max(own, y_rank), x_size + layers * y_size), bf16)],
        [VMEM] * (1 + owners),
        scratch=[pltpu.VMEM((layers, y_size, group * rank), bf16)],
    )(y_factor.T, *received)[0]
    payloads = [payload] + [lax.ppermute(payload, "ga", ring_pairs(n_a, k)) for k in range(1, n_a)]
    x_gram, products = call(
        functools.partial(last_kernel, x_size, n_a),
        [sds((own, x_size), f32), sds((layers, y_rank, y_size), f32)],
        [VMEM] * n_a,
        limit=8,
    )(*payloads)
    return (
        new_fields.reshape(fields.shape),
        x_gram,
        jnp.swapaxes(products, 1, 2),
    )


def solution(mesh):
    block = P(None, "gy", "gz", "ga")
    in_specs = (block, block, block, P(), P(), P(), P())
    out_specs = (block, P(("gy", "gz"), None), P(("gz", "gy"), None, None))

    return jax.shard_map(shards, mesh=mesh, in_specs=in_specs, out_specs=out_specs, check_vma=False)
```

```python
import functools

import jax
import jax.numpy as jnp
from jax import lax
from jax.experimental import pallas as pl
from jax.experimental.pallas import tpu as pltpu
from jax.sharding import PartitionSpec as P


time_step = 0.4
old_share, new_share = 0.75, 0.25
TILE = 32
SUB = 16
VMEM = pl.BlockSpec(memory_space=pltpu.VMEM)
SMEM = pl.BlockSpec(memory_space=pltpu.SMEM)
ANY = pl.BlockSpec(memory_space=pl.ANY)
f32, bf16 = jnp.float32, jnp.bfloat16
sds = jax.ShapeDtypeStruct
MIB = 1024 * 1024


def swap_pairs(count, turn):
    if turn == 0:
        return [(i, i ^ 1) for i in range(count)]
    return [(i, (i + (1 if i % 2 else -1)) % count) for i in range(count)]


def origin(count, index, step):
    if count & (count - 1) == 0:
        return index ^ step
    return (index - step + count) % count


def turns(count):
    return 1 if count == 2 else 2


def ring_pairs(count, step):
    return [(i, (i + step) % count) for i in range(count)]


def corner_mask(lanes):
    row = lax.broadcasted_iota(jnp.int32, (8, lanes), 0)
    lane = lax.broadcasted_iota(jnp.int32, (8, lanes), 1)
    return jnp.where(
        ((row == 0) & (lane == 0)) | ((row == 1) & (lane == lanes - 1)), 1.0, 0.0
    ).astype(bf16)


def rows_of(ref, v, segments):
    return jnp.concatenate([ref[v, first : first + count, :] for first, count in segments], axis=0)


def pack_kernel(z_cells, counts, plan, f_hbm, *refs):
    f_ref, outs, sem = refs[0], refs[1:-1], refs[-1]
    variables, rows, lanes = f_ref.shape
    n_y, n_z, n_a = counts
    n_sem = sem.shape[0]
    step = variables // n_sem
    loads = [
        pltpu.make_async_copy(
            f_hbm.at[pl.ds(i * step, step)], f_ref.at[pl.ds(i * step, step)], sem.at[i]
        )
        for i in range(n_sem)
    ]
    for load in loads:
        load.start()
    y_refs, outs = outs[: turns(n_y)], outs[turns(n_y) :]
    x_refs, z_refs = outs[: turns(n_a)], outs[turns(n_a) :]
    odd_y, odd_z, odd_a = (lax.rem(lax.axis_index(a), 2) for a in ("gy", "gz", "ga"))
    pick = corner_mask(lanes)
    for v in range(variables):
        if v % step == 0:
            loads[v // step].wait()
        for c, segments in enumerate(plan):
            size = sum(count for _, count in segments)
            at = 0
            for first, count in segments:
                y_count = count // z_cells
                for turn in range(turns(n_z)):
                    start = first + jnp.where(odd_z == turn, z_cells - 1, 0)
                    z_refs[c * turns(n_z) + turn][v, at : at + y_count, :] = f_ref[
                        v, pl.ds(start, y_count, stride=z_cells), :
                    ].astype(bf16)
                at += y_count
            edges = lax.dot_general(
                pick, rows_of(f_ref, v, segments).astype(bf16), (((1,), (1,)), ((), ())),
                preferred_element_type=f32,
            )
            for turn in range(turns(n_a)):
                x_refs[turn][c : c + 1, v * size : (v + 1) * size] = jnp.where(
                    odd_a == turn, edges[1:2, :], edges[0:1, :]
                )
        for turn in range(turns(n_y)):
            y_refs[turn][v] = jnp.where(
                odd_y == turn, f_ref[v, rows - z_cells :, :], f_ref[v, :z_cells, :]
            )


def low_high(axis, count, halos):
    index = lax.axis_index(axis)
    odd = lax.rem(index, 2)
    a, b = halos[0], halos[-1]

    def pick(value_of):
        first, second = value_of(a), value_of(b)
        low = jnp.where(odd == 1, first, second)
        high = jnp.where(odd == 1, second, first)
        zero = jnp.zeros_like(low)
        return jnp.where(index > 0, low, zero), jnp.where(index < count - 1, high, zero)

    return pick


def mix_kernel(r_ref, vel_hbm, after, out_ref, vel_ref, sem):
    load = pltpu.make_async_copy(vel_hbm, vel_ref, sem)
    load.start()
    count = r_ref.shape[0]
    size = out_ref.shape[0]
    spread = jnp.where(
        lax.broadcasted_iota(jnp.int32, (size, count), 0) // SUB
        == lax.broadcasted_iota(jnp.int32, (size, count), 1),
        1.0,
        0.0,
    ).astype(bf16)
    scaled = (r_ref[...] * (new_share * time_step)).astype(bf16)
    left = lax.dot_general(spread, scaled, (((1,), (0,)), ((), ())), preferred_element_type=f32)
    both = lax.dot_general(
        left.astype(bf16), spread, (((1,), (1,)), ((), ())), preferred_element_type=f32
    )
    row = lax.broadcasted_iota(jnp.int32, (size, size), 0)
    col = lax.broadcasted_iota(jnp.int32, (size, size), 1)
    out_ref[...] = jnp.where(row % SUB == col % SUB, both, 0.0).astype(bf16)
    load.wait()


def stencil_kernel(
    z_cells, counts, index, segments, has_y, diffusion, vel_ref, start_ref, f_ref, mix_ref, *rest
):
    n_y, n_z, parts = counts
    x_refs, rest = rest[: turns(parts)], rest[turns(parts) :]
    z_refs, rest = rest[: turns(n_z)], rest[turns(n_z) :]
    if has_y:
        y_refs, rest = rest[: turns(n_y)], rest[turns(n_y) :]
    new_ref, rest = rest[0], rest[1:]
    snaps, (ends, edge, zface, react) = rest[:parts], rest[parts:]
    variables, rows, lanes = f_ref.shape
    pad = -(-z_cells // 8) * 8
    tile = TILE
    chunk = sum(count for _, count in segments)
    me = lax.axis_index("ga")
    is_buffer = me == parts - 1

    tile_rows = [first + k * tile for first, count in segments for k in range(count // tile)]

    put = corner_mask(lanes)
    side = lax.broadcasted_iota(jnp.int32, (8, chunk), 0)
    y_count = chunk // z_cells
    x_pair = low_high("ga", parts, x_refs)
    z_pair = low_high("gz", n_z, z_refs)
    for v in range(variables):
        first, second = x_pair(lambda ref: ref[index : index + 1, v * chunk : (v + 1) * chunk])
        first = jnp.broadcast_to(first, (8, chunk))
        second = jnp.broadcast_to(second, (8, chunk))
        both = jnp.where(side == 0, first, jnp.where(side == 1, second, 0.0)).astype(bf16)
        edge[v] = lax.dot_general(both, put, (((0,), (0,)), ((), ())), preferred_element_type=f32)
        first, second = z_pair(lambda ref: ref[v].astype(f32))
        zface[v, pl.ds(0, y_count, stride=z_cells), :] = first
        zface[v, pl.ds(z_cells - 1, y_count, stride=z_cells), :] = second
    if has_y:
        low, high = low_high("gy", n_y, y_refs)(lambda ref: ref[...])
        ends[0, :, pad - z_cells : pad, :] = low
        ends[0, :, pad:, :] = f_ref[:, : tile + pad, :]
        ends[1, :, : tile + pad, :] = f_ref[:, rows - tile - pad :, :]
        ends[1, :, tile + pad : tile + pad + z_cells, :] = high

    rate = new_share * time_step
    group = variables // parts
    lane = lax.broadcasted_iota(jnp.int32, (SUB, lanes), 1)
    z_at = lax.rem(lax.broadcasted_iota(jnp.int32, (SUB, lanes), 0), z_cells)
    for t, row in enumerate(tile_rows):
        slot = t % 2
        blocks = []
        for sub in range(tile // SUB):
            at = row + sub * SUB
            blocks.append(
                jnp.concatenate([f_ref[w, at : at + SUB, :].astype(bf16) for w in range(variables)], axis=0)
            )
        react[slot] = jnp.dot(mix_ref[...], jnp.concatenate(blocks, axis=1), preferred_element_type=f32)
        for sub in range(tile // SUB):
            at, here = row + sub * SUB, t * tile + sub * SUB

            def rows_at(v, offset):
                if row == 0:
                    return ends[0, v, pad + sub * SUB + offset : pad + (sub + 1) * SUB + offset, :]
                if row == rows - tile:
                    return ends[1, v, pad + sub * SUB + offset : pad + (sub + 1) * SUB + offset, :]
                return f_ref[v, at + offset : at + SUB + offset, :]

            v_x = vel_ref[0, at : at + SUB, :] * (0.5 * rate)
            v_y = vel_ref[1, at : at + SUB, :] * (0.5 * rate)
            v_z = vel_ref[2, at : at + SUB, :] * (0.5 * rate)
            for part in range(parts):
                target = lax.rem(me + part, parts)
                for j in range(group):
                    v = target * group + j
                    spread = diffusion[v] * rate
                    center = rows_at(v, 0)
                    y_minus = rows_at(v, -z_cells)
                    y_plus = rows_at(v, z_cells)
                    face = zface[v, here : here + SUB, :]
                    z_minus = jnp.where(z_at == 0, face, rows_at(v, -1))
                    z_plus = jnp.where(z_at == z_cells - 1, face, rows_at(v, 1))
                    sides = edge[v, here : here + SUB, :]
                    x_minus = jnp.where(lane == 0, sides, pltpu.roll(center, 1, 1))
                    x_plus = jnp.where(lane == lanes - 1, sides, pltpu.roll(center, lanes - 1, 1))
                    mixed = react[
                        slot, pl.ds(pl.multiple_of(v * SUB, SUB), SUB), sub * lanes : (sub + 1) * lanes
                    ]
                    around = (y_plus + y_minus) + (z_plus + z_minus) + (x_plus + x_minus)
                    carried = (
                        v_x * (x_plus - x_minus) + v_y * (y_plus - y_minus) + v_z * (z_plus - z_minus)
                    )
                    value = (
                        old_share * start_ref[v, at : at + SUB, :]
                        + (new_share - 6.0 * spread) * center
                        + (spread * around - carried)
                        + mixed
                    )
                    value = jnp.where(is_buffer, center, value)
                    new_ref[v, here : here + SUB, :] = value
                    snaps[part][j, here : here + SUB, :] = value.astype(bf16)


def flush_kernel(plan, *refs):
    parts, (new_hbm, sem) = refs[: len(plan)], refs[len(plan) :]
    writes = []
    for part, segments in zip(parts, plan):
        at = 0
        for first, count in segments:
            writes.append(
                pltpu.make_async_copy(
                    part.at[:, pl.ds(at, count), :], new_hbm.at[:, pl.ds(first, count), :], sem.at[len(writes)]
                )
            )
            writes[-1].start()
            at += count
    for write in writes:
        write.wait()


def gather_rows(parts, me, pieces, wide):
    group, rows, lanes = pieces[0].shape
    for part in range(parts):
        source = lax.rem(me - part + parts, parts)
        at = pl.multiple_of(source * lanes, lanes)
        for j in range(group):
            wide[j * rows : (j + 1) * rows, pl.ds(at, lanes)] = pieces[part][j]


def project(z_cells, group, rows, xf_ref, wide, proj, store):
    y_cells = rows // z_cells
    proj[...] = lax.dot_general(
        wide[...], xf_ref[...], (((1,), (1,)), ((), ())), preferred_element_type=f32
    )
    for z in range(z_cells):
        cols = [proj[pl.ds(j * rows + z, y_cells, stride=z_cells), :] for j in range(group)]
        store(z, jnp.concatenate(cols, axis=1).astype(bf16))


def part_gram_kernel(z_cells, parts, has_prior, xf_ref, *refs):
    pieces, refs = refs[:parts], refs[parts:]
    if has_prior:
        prior, refs = refs[0], refs[1:]
    gram_ref, proj_ref, wide, proj = refs
    group, rows, _ = pieces[0].shape
    gather_rows(parts, lax.axis_index("ga"), pieces, wide)
    data = wide[...]
    gram = lax.dot_general(data, data, (((0,), (0,)), ((), ())), preferred_element_type=f32)
    gram_ref[...] = prior[...] + gram if has_prior else gram

    def store(z, value):
        proj_ref[z] = value

    project(z_cells, group, rows, xf_ref, wide, proj, store)


def last_gram_kernel(z_cells, parts, n_y, n_z, plan, xf_ref, *refs):
    priors = len(plan) - 1
    pieces, refs = refs[:parts], refs[parts:]
    prior, refs = refs[0], refs[1:]
    prior_proj, refs = refs[:priors], refs[priors:]
    outs, (wide, proj, gram, full) = refs[:2], refs[2:]
    group, rows, _ = pieces[0].shape
    me, my_y, my_z = (lax.axis_index(a) for a in ("ga", "gy", "gz"))
    gather_rows(parts, me, pieces, wide)

    def place(z, value, segments):
        at = 0
        for first, count in segments:
            y_count = count // z_cells
            full[z, first // z_cells : first // z_cells + y_count, :] = value[at : at + y_count]
            at += y_count

    project(z_cells, group, rows, xf_ref, wide, proj, lambda z, value: place(z, value, plan[-1]))
    for i in range(priors):
        for z in range(z_cells):
            place(z, prior_proj[i][z], plan[i])
    data = wide[...]
    gram[...] = prior[...] + lax.dot_general(
        data, data, (((0,), (0,)), ((), ())), preferred_element_type=f32
    )
    own = gram.shape[0] // (n_y * n_z)
    width = gram.shape[1]
    layers = z_cells // n_y
    cols = full.shape[2]
    y_cells = full.shape[1]
    for flip, out in enumerate(outs):
        out[...] = jnp.zeros_like(out)
        for d_x in range(n_y // 2):
            for d_z in range(n_z):
                block = d_x * n_z + d_z
                y_to, z_to = my_y ^ (2 * d_x + flip), my_z ^ d_z
                at = pl.multiple_of((y_to * n_z + z_to) * own, own)
                out[block, :own, :width] = gram[pl.ds(at, own), :].astype(bf16)
                if d_z == 0:
                    for layer in range(layers):
                        out[block, :y_cells, width + layer * cols : width + (layer + 1) * cols] = full[
                            y_to * layers + layer
                        ]


def pair_kernel(n_z, own, width, keep_ref, other_ref, *outs):
    for block, out in enumerate(outs):
        both = keep_ref[block, :own, :width].astype(f32) + other_ref[block, :own, :width].astype(f32)
        if block % n_z:
            out[...] = both.astype(bf16)
        else:
            side = keep_ref.shape[2] - width
            if out.shape[0] != own:
                out[...] = jnp.zeros_like(out)
            out[:own, :width] = both.astype(bf16)
            out[:, width : width + side] = keep_ref[block, :, width:]
            out[:, width + side :] = other_ref[block, :, width:]


def layer_kernel(n_y, n_z, paired, own, layers, y_scale, x_scale, yf_ref, *refs):
    pieces, (out_ref, m_ref) = refs[:-2], refs[-2:]
    rank, y_size = yf_ref.shape
    y_cells = y_size // n_y
    cols = m_ref.shape[2]
    senders = 2 if paired else 1
    width = pieces[0].shape[1] - senders * layers * cols
    my_y = lax.axis_index("gy")
    for d in range(n_y // senders):
        for sender in range(senders):
            source = my_y ^ (2 * d + sender) if paired else origin(n_y, my_y, d)
            at = pl.multiple_of(source * y_cells, y_cells)
            for layer in range(layers):
                start = width + (sender * layers + layer) * cols
                m_ref[layer, pl.ds(at, y_cells), :] = pieces[d * n_z][:y_cells, start : start + cols]
    for layer in range(layers):
        m = m_ref[layer]
        y_gram = lax.dot_general(m, m, (((1,), (1,)), ((), ())), preferred_element_type=f32) * y_scale
        prod = lax.dot_general(
            yf_ref[...], y_gram, (((1,), (0,)), ((), ())), preferred_element_type=f32,
            precision=lax.Precision.HIGHEST,
        )
        if own != rank:
            out_ref[...] = jnp.zeros_like(out_ref)
        out_ref[:rank, width + layer * y_size : width + (layer + 1) * y_size] = prod.astype(bf16)
    total = pieces[0][:own, :width].astype(f32)
    for piece in pieces[1:]:
        total = total + piece[:own, :width].astype(f32)
    out_ref[:own, :width] = (total * x_scale).astype(bf16)


def last_kernel(width, parts, *refs):
    pieces, (gram_ref, prod_ref) = refs[:parts], refs[parts:]
    total = pieces[0][...].astype(f32)
    for i in range(1, parts):
        total = total + pieces[i][...].astype(f32)
    gram_ref[...] = total[: gram_ref.shape[0], :width]
    layers, rank, y_size = prod_ref.shape
    for layer in range(layers):
        prod_ref[layer] = total[:rank, width + layer * y_size : width + (layer + 1) * y_size]


def call(kernel, out_shapes, in_specs, scratch=(), limit=16, flops=0, moved=0):
    return pl.pallas_call(
        kernel,
        out_shape=out_shapes,
        in_specs=in_specs,
        out_specs=[VMEM] * len(out_shapes),
        scratch_shapes=list(scratch),
        cost_estimate=pl.CostEstimate(flops=flops, bytes_accessed=moved, transcendentals=0),
        compiler_params=pltpu.CompilerParams(vmem_limit_bytes=limit * MIB),
    )


def shards(fields, section_start, velocity, diffusivity, reaction, x_factor, y_factor):
    variables, y_cells, z_cells, lanes = fields.shape
    rows = y_cells * z_cells
    n_y, n_z, n_a = (lax.axis_size(a) for a in ("gy", "gz", "ga"))
    g_y, g_z, _ = (lax.axis_index(a) for a in ("gy", "gz", "ga"))
    f = fields.reshape(variables, rows, lanes)
    s = section_start.reshape(variables, rows, lanes)
    vel = velocity.reshape(3, rows, lanes)
    x_size = n_a * lanes
    y_size = n_y * y_cells
    rank, y_rank = x_factor.shape[1], y_factor.shape[1]
    group = variables // n_a
    owners = n_y * n_z
    own = x_size // owners
    layers = z_cells // n_y
    pad = -(-z_cells // 8) * 8
    tile = TILE
    quarter = rows // 4
    plan = (((quarter, 2 * quarter),), ((0, quarter), (3 * quarter, quarter)))
    chunk = 2 * quarter
    y_part = chunk // z_cells
    counts = (n_y, n_z, n_a)
    in_hbm = functools.partial(pltpu.with_memory_space_constraint, memory_space=pltpu.HBM)
    packed = call(
        functools.partial(pack_kernel, z_cells, counts, plan),
        [sds((variables, rows, lanes), f32)]
        + [sds((variables, z_cells, lanes), f32)] * turns(n_y)
        + [sds((len(plan), variables * chunk), f32)] * turns(n_a)
        + [sds((variables, y_part, lanes), bf16)] * (turns(n_z) * len(plan)),
        [ANY],
        scratch=[pltpu.SemaphoreType.DMA((min(variables, 8),))],
        limit=12,
    )(in_hbm(f))
    f, packed = packed[0], packed[1:]
    y_faces, packed = packed[: turns(n_y)], packed[turns(n_y) :]
    x_edges, z_faces = packed[: turns(n_a)], packed[turns(n_a) :]

    def halo(axis, count, faces):
        received = []
        for turn, face in enumerate(faces):
            received.append(lax.ppermute(face, axis, swap_pairs(count, turn)))
        return received

    mix, vel = call(
        mix_kernel,
        [sds((variables * SUB, variables * SUB), bf16), sds(vel.shape, f32)],
        [VMEM, ANY, ANY],
        scratch=[pltpu.SemaphoreType.DMA],
        limit=8,
    )(reaction, in_hbm(vel), y_faces[0])

    def stencil(index, x_halos, z_halos, y_halos):
        segments = plan[index]
        operands = [diffusivity, vel, s, f, mix, *x_halos, *z_halos, *y_halos]
        return pl.pallas_call(
            functools.partial(stencil_kernel, z_cells, counts, index, segments, bool(y_halos)),
            out_shape=[sds((variables, chunk, lanes), f32)] + [sds((group, chunk, lanes), bf16)] * n_a,
            in_specs=[SMEM] + [VMEM] * (len(operands) - 1),
            out_specs=[VMEM] * (n_a + 1),
            scratch_shapes=[
                pltpu.VMEM((2, variables, tile + 2 * pad, lanes), f32),
                pltpu.VMEM((variables, chunk, lanes), f32),
                pltpu.VMEM((variables, chunk, lanes), f32),
                pltpu.VMEM((2, variables * SUB, tile // SUB * lanes), f32),
            ],
            name="stencil",
            compiler_params=pltpu.CompilerParams(vmem_limit_bytes=20 * MIB),
        )(*operands)

    def exchange(snaps):
        received = [snaps[0]]
        for k in range(1, n_a):
            received.append(lax.ppermute(snaps[k], "ga", ring_pairs(n_a, k)))
        return received

    early_z, late_z = z_faces[: turns(n_z)], z_faces[turns(n_z) :]
    z_halos = halo("gz", n_z, early_z)
    x_halos = halo("ga", n_a, x_edges)
    y_halos = halo("gy", n_y, y_faces)
    results = stencil(0, x_halos, z_halos, ())
    news = [results[0]]
    chunks = [exchange(results[1:])]
    late_z, _ = lax.optimization_barrier((tuple(late_z), results[2]))
    z_halos = halo("gz", n_z, late_z)
    results = stencil(1, x_halos, z_halos, y_halos)
    news.append(results[0])
    chunks.append(exchange(results[1:]))
    new_fields = pl.pallas_call(
        functools.partial(flush_kernel, plan),
        out_shape=sds((variables, rows, lanes), f32),
        in_specs=[VMEM] * len(plan),
        out_specs=ANY,
        scratch_shapes=[pltpu.SemaphoreType.DMA((sum(len(segments) for segments in plan),))],
        name="flush",
        compiler_params=pltpu.CompilerParams(vmem_limit_bytes=4 * MIB),
    )(*news)

    scratch = [pltpu.VMEM((group * chunk, x_size), bf16), pltpu.VMEM((group * chunk, rank), f32)]
    gram, projs = None, []
    direct = owners <= 8 and n_y in (2, 4, 8) and n_z in (1, 2, 4)
    for index in range(len(plan) - 1 if direct else len(plan)):
        gram, proj = call(
            functools.partial(part_gram_kernel, z_cells, n_a, gram is not None),
            [sds((x_size, x_size), f32), sds((z_cells, y_part, group * rank), bf16)],
            [VMEM] * (n_a + 1 + (gram is not None)),
            scratch=scratch,
        )(x_factor.T, *chunks[index], *([] if gram is None else [gram]))
        projs.append(proj)
    cols = layers * group * rank
    piece_rows = max(own, y_cells)
    if direct:
        blocks = n_y // 2 * n_z
        keep, send = call(
            functools.partial(last_gram_kernel, z_cells, n_a, n_y, n_z, plan),
            [sds((blocks, piece_rows, x_size + cols), bf16)] * 2,
            [VMEM] * (n_a + 2 + len(projs)),
            scratch=scratch
            + [pltpu.VMEM((x_size, x_size), f32), pltpu.VMEM((z_cells, y_cells, group * rank), bf16)],
        )(x_factor.T, *chunks[-1], gram, *projs)
        other = lax.ppermute(send, "gy", swap_pairs(n_y, 0))
        sums = call(
            functools.partial(pair_kernel, n_z, own, x_size),
            [
                sds((own, x_size), bf16) if block % n_z else sds((piece_rows, x_size + 2 * cols), bf16)
                for block in range(blocks)
            ],
            [VMEM] * 2,
        )(keep, other)
        received = [sums[0]]
        for block in range(1, blocks):
            d_x, d_z = block // n_z, block % n_z
            pairs = [
                (y * n_z + z, (y ^ (2 * d_x)) * n_z + (z ^ d_z)) for y in range(n_y) for z in range(n_z)
            ]
            received.append(lax.ppermute(sums[block], ("gy", "gz"), pairs))
    else:
        half = quarter // z_cells
        proj = jnp.concatenate([projs[1][:, :half], projs[0], projs[1][:, half:]], axis=1)
        full = lax.all_to_all(
            proj.reshape(n_y, layers, y_cells, group * rank), "gy", split_axis=0, concat_axis=0, tiled=True
        )
        blocks = lax.all_to_all(
            gram.astype(bf16).reshape(owners, own, x_size), ("gy", "gz"), split_axis=0, concat_axis=0, tiled=True
        )
        full = full.transpose(0, 2, 1, 3).reshape(n_y, y_cells, cols)
        received = []
        for d_y in range(n_y):
            for d_z in range(n_z):
                source = origin(n_y, g_y, d_y) * n_z + origin(n_z, g_z, d_z)
                block = lax.dynamic_index_in_dim(blocks, source, 0, keepdims=False)
                if d_z == 0:
                    block = jnp.pad(block, ((0, piece_rows - own), (0, 0)))
                    side = lax.dynamic_index_in_dim(full, origin(n_y, g_y, d_y), 0, keepdims=False)
                    side = jnp.pad(side, ((0, piece_rows - y_cells), (0, 0)))
                    block = jnp.concatenate([block, side], axis=1)
                received.append(block)
    payload = call(
        functools.partial(
            layer_kernel, n_y, n_z, direct, own, layers, 1.0 / (variables * rank), 1.0 / (variables * rows * owners)
        ),
        [sds((max(own, y_rank), x_size + layers * y_size), bf16)],
        [VMEM] * (1 + len(received)),
        scratch=[pltpu.VMEM((layers, y_size, group * rank), bf16)],
    )(y_factor.T, *received)[0]
    payloads = [payload] + [lax.ppermute(payload, "ga", ring_pairs(n_a, k)) for k in range(1, n_a)]
    x_gram, products = call(
        functools.partial(last_kernel, x_size, n_a),
        [sds((own, x_size), f32), sds((layers, y_rank, y_size), f32)],
        [VMEM] * n_a,
        limit=8,
    )(*payloads)
    return (
        new_fields.reshape(fields.shape),
        x_gram,
        jnp.swapaxes(products, 1, 2),
    )


def solution(mesh):
    block = P(None, "gy", "gz", "ga")
    in_specs = (block, block, block, P(), P(), P(), P())
    out_specs = (block, P(("gy", "gz"), None), P(("gz", "gy"), None, None))

    return jax.shard_map(shards, mesh=mesh, in_specs=in_specs, out_specs=out_specs, check_vma=False)
```

```python
import functools

import jax
import jax.numpy as jnp
from jax import lax
from jax.experimental import pallas as pl
from jax.experimental.pallas import tpu as pltpu
from jax.sharding import PartitionSpec as P


time_step = 0.4
old_share, new_share = 0.75, 0.25
TILE = 32
SUB = 16
VMEM = pl.BlockSpec(memory_space=pltpu.VMEM)
SMEM = pl.BlockSpec(memory_space=pltpu.SMEM)
ANY = pl.BlockSpec(memory_space=pl.ANY)
f32, bf16 = jnp.float32, jnp.bfloat16
sds = jax.ShapeDtypeStruct
MIB = 1024 * 1024


def swap_pairs(count, turn):
    if turn == 0:
        return [(i, i ^ 1) for i in range(count)]
    return [(i, (i + (1 if i % 2 else -1)) % count) for i in range(count)]


def partner(count, index, step):
    if count & (count - 1) == 0:
        return index ^ step
    return (index + step) % count


def origin(count, index, step):
    if count & (count - 1) == 0:
        return index ^ step
    return (index - step + count) % count


def turns(count):
    return 1 if count == 2 else 2


def ring_pairs(count, step):
    return [(i, (i + step) % count) for i in range(count)]


def corner_mask(lanes):
    row = lax.broadcasted_iota(jnp.int32, (8, lanes), 0)
    lane = lax.broadcasted_iota(jnp.int32, (8, lanes), 1)
    return jnp.where(
        ((row == 0) & (lane == 0)) | ((row == 1) & (lane == lanes - 1)), 1.0, 0.0
    ).astype(bf16)


def rows_of(ref, v, segments):
    return jnp.concatenate([ref[v, first : first + count, :] for first, count in segments], axis=0)


def pack_kernel(z_cells, counts, plan, f_hbm, *refs):
    f_ref, outs, sem = refs[0], refs[1:-1], refs[-1]
    variables, rows, lanes = f_ref.shape
    n_y, n_z, n_a = counts
    n_sem = sem.shape[0]
    step = variables // n_sem
    loads = [
        pltpu.make_async_copy(
            f_hbm.at[pl.ds(i * step, step)], f_ref.at[pl.ds(i * step, step)], sem.at[i]
        )
        for i in range(n_sem)
    ]
    for load in loads:
        load.start()
    y_refs, outs = outs[: turns(n_y)], outs[turns(n_y) :]
    x_refs, z_refs = outs[: turns(n_a)], outs[turns(n_a) :]
    odd_y, odd_z, odd_a = (lax.rem(lax.axis_index(a), 2) for a in ("gy", "gz", "ga"))
    pick = corner_mask(lanes)
    for v in range(variables):
        if v % step == 0:
            loads[v // step].wait()
        for c, segments in enumerate(plan):
            size = sum(count for _, count in segments)
            at = 0
            for first, count in segments:
                y_count = count // z_cells
                for turn in range(turns(n_z)):
                    start = first + jnp.where(odd_z == turn, z_cells - 1, 0)
                    z_refs[c * turns(n_z) + turn][v, at : at + y_count, :] = f_ref[
                        v, pl.ds(start, y_count, stride=z_cells), :
                    ].astype(bf16)
                at += y_count
            edges = lax.dot_general(
                pick, rows_of(f_ref, v, segments).astype(bf16), (((1,), (1,)), ((), ())),
                preferred_element_type=f32,
            )
            for turn in range(turns(n_a)):
                x_refs[turn][c : c + 1, v * size : (v + 1) * size] = jnp.where(
                    odd_a == turn, edges[1:2, :], edges[0:1, :]
                )
        for turn in range(turns(n_y)):
            y_refs[turn][v] = jnp.where(
                odd_y == turn, f_ref[v, rows - z_cells :, :], f_ref[v, :z_cells, :]
            )


def low_high(axis, count, halos):
    index = lax.axis_index(axis)
    odd = lax.rem(index, 2)
    a, b = halos[0], halos[-1]

    def pick(value_of):
        first, second = value_of(a), value_of(b)
        low = jnp.where(odd == 1, first, second)
        high = jnp.where(odd == 1, second, first)
        zero = jnp.zeros_like(low)
        return jnp.where(index > 0, low, zero), jnp.where(index < count - 1, high, zero)

    return pick


def mix_kernel(r_ref, vel_hbm, after, out_ref, vel_ref, sem):
    load = pltpu.make_async_copy(vel_hbm, vel_ref, sem)
    load.start()
    count = r_ref.shape[0]
    size = out_ref.shape[0]
    spread = jnp.where(
        lax.broadcasted_iota(jnp.int32, (size, count), 0) // SUB
        == lax.broadcasted_iota(jnp.int32, (size, count), 1),
        1.0,
        0.0,
    ).astype(bf16)
    scaled = (r_ref[...] * (new_share * time_step)).astype(bf16)
    left = lax.dot_general(spread, scaled, (((1,), (0,)), ((), ())), preferred_element_type=f32)
    both = lax.dot_general(
        left.astype(bf16), spread, (((1,), (1,)), ((), ())), preferred_element_type=f32
    )
    row = lax.broadcasted_iota(jnp.int32, (size, size), 0)
    col = lax.broadcasted_iota(jnp.int32, (size, size), 1)
    out_ref[...] = jnp.where(row % SUB == col % SUB, both, 0.0).astype(bf16)
    load.wait()


def stencil_kernel(
    z_cells, counts, index, segments, has_y, diffusion, vel_ref, start_ref, f_ref, mix_ref, *rest
):
    n_y, n_z, parts = counts
    x_refs, rest = rest[: turns(parts)], rest[turns(parts) :]
    z_refs, rest = rest[: turns(n_z)], rest[turns(n_z) :]
    if has_y:
        y_refs, rest = rest[: turns(n_y)], rest[turns(n_y) :]
    new_ref, rest = rest[0], rest[1:]
    snaps, (ends, edge, zface, react) = rest[:parts], rest[parts:]
    variables, rows, lanes = f_ref.shape
    pad = -(-z_cells // 8) * 8
    tile = TILE
    chunk = sum(count for _, count in segments)
    me = lax.axis_index("ga")
    is_buffer = me == parts - 1

    tile_rows = [first + k * tile for first, count in segments for k in range(count // tile)]

    put = corner_mask(lanes)
    side = lax.broadcasted_iota(jnp.int32, (8, chunk), 0)
    y_count = chunk // z_cells
    x_pair = low_high("ga", parts, x_refs)
    z_pair = low_high("gz", n_z, z_refs)
    for v in range(variables):
        first, second = x_pair(lambda ref: ref[index : index + 1, v * chunk : (v + 1) * chunk])
        first = jnp.broadcast_to(first, (8, chunk))
        second = jnp.broadcast_to(second, (8, chunk))
        both = jnp.where(side == 0, first, jnp.where(side == 1, second, 0.0)).astype(bf16)
        edge[v] = lax.dot_general(both, put, (((0,), (0,)), ((), ())), preferred_element_type=f32)
        first, second = z_pair(lambda ref: ref[v].astype(f32))
        zface[v, pl.ds(0, y_count, stride=z_cells), :] = first
        zface[v, pl.ds(z_cells - 1, y_count, stride=z_cells), :] = second
    if has_y:
        low, high = low_high("gy", n_y, y_refs)(lambda ref: ref[...])
        ends[0, :, pad - z_cells : pad, :] = low
        ends[0, :, pad:, :] = f_ref[:, : tile + pad, :]
        ends[1, :, : tile + pad, :] = f_ref[:, rows - tile - pad :, :]
        ends[1, :, tile + pad : tile + pad + z_cells, :] = high

    rate = new_share * time_step
    group = variables // parts
    lane = lax.broadcasted_iota(jnp.int32, (SUB, lanes), 1)
    z_at = lax.rem(lax.broadcasted_iota(jnp.int32, (SUB, lanes), 0), z_cells)
    for t, row in enumerate(tile_rows):
        slot = t % 2
        blocks = []
        for sub in range(tile // SUB):
            at = row + sub * SUB
            blocks.append(
                jnp.concatenate([f_ref[w, at : at + SUB, :].astype(bf16) for w in range(variables)], axis=0)
            )
        react[slot] = jnp.dot(mix_ref[...], jnp.concatenate(blocks, axis=1), preferred_element_type=f32)
        for sub in range(tile // SUB):
            at, here = row + sub * SUB, t * tile + sub * SUB

            def rows_at(v, offset):
                if row == 0:
                    return ends[0, v, pad + sub * SUB + offset : pad + (sub + 1) * SUB + offset, :]
                if row == rows - tile:
                    return ends[1, v, pad + sub * SUB + offset : pad + (sub + 1) * SUB + offset, :]
                return f_ref[v, at + offset : at + SUB + offset, :]

            v_x = vel_ref[0, at : at + SUB, :] * (0.5 * rate)
            v_y = vel_ref[1, at : at + SUB, :] * (0.5 * rate)
            v_z = vel_ref[2, at : at + SUB, :] * (0.5 * rate)
            for part in range(parts):
                target = lax.rem(me + part, parts)
                for j in range(group):
                    v = target * group + j
                    spread = diffusion[v] * rate
                    center = rows_at(v, 0)
                    y_minus = rows_at(v, -z_cells)
                    y_plus = rows_at(v, z_cells)
                    face = zface[v, here : here + SUB, :]
                    z_minus = jnp.where(z_at == 0, face, rows_at(v, -1))
                    z_plus = jnp.where(z_at == z_cells - 1, face, rows_at(v, 1))
                    sides = edge[v, here : here + SUB, :]
                    x_minus = jnp.where(lane == 0, sides, pltpu.roll(center, 1, 1))
                    x_plus = jnp.where(lane == lanes - 1, sides, pltpu.roll(center, lanes - 1, 1))
                    mixed = react[
                        slot, pl.ds(pl.multiple_of(v * SUB, SUB), SUB), sub * lanes : (sub + 1) * lanes
                    ]
                    around = (y_plus + y_minus) + (z_plus + z_minus) + (x_plus + x_minus)
                    carried = (
                        v_x * (x_plus - x_minus) + v_y * (y_plus - y_minus) + v_z * (z_plus - z_minus)
                    )
                    value = (
                        old_share * start_ref[v, at : at + SUB, :]
                        + (new_share - 6.0 * spread) * center
                        + (spread * around - carried)
                        + mixed
                    )
                    value = jnp.where(is_buffer, center, value)
                    new_ref[v, here : here + SUB, :] = value
                    snaps[part][j, here : here + SUB, :] = value.astype(bf16)


def flush_kernel(plan, *refs):
    parts, (new_hbm, sem) = refs[: len(plan)], refs[len(plan) :]
    writes = []
    for part, segments in zip(parts, plan):
        at = 0
        for first, count in segments:
            writes.append(
                pltpu.make_async_copy(
                    part.at[:, pl.ds(at, count), :], new_hbm.at[:, pl.ds(first, count), :], sem.at[len(writes)]
                )
            )
            writes[-1].start()
            at += count
    for write in writes:
        write.wait()


def gather_rows(parts, me, pieces, wide):
    group, rows, lanes = pieces[0].shape
    for part in range(parts):
        source = lax.rem(me - part + parts, parts)
        at = pl.multiple_of(source * lanes, lanes)
        for j in range(group):
            wide[j * rows : (j + 1) * rows, pl.ds(at, lanes)] = pieces[part][j]


def project(z_cells, group, rows, xf_ref, wide, proj, store):
    y_cells = rows // z_cells
    proj[...] = lax.dot_general(
        wide[...], xf_ref[...], (((1,), (1,)), ((), ())), preferred_element_type=f32
    )
    for z in range(z_cells):
        cols = [proj[pl.ds(j * rows + z, y_cells, stride=z_cells), :] for j in range(group)]
        store(z, jnp.concatenate(cols, axis=1).astype(bf16))


def part_gram_kernel(z_cells, parts, has_prior, xf_ref, *refs):
    pieces, refs = refs[:parts], refs[parts:]
    if has_prior:
        prior, refs = refs[0], refs[1:]
    gram_ref, proj_ref, wide, proj = refs
    group, rows, _ = pieces[0].shape
    gather_rows(parts, lax.axis_index("ga"), pieces, wide)
    data = wide[...]
    gram = lax.dot_general(data, data, (((0,), (0,)), ((), ())), preferred_element_type=f32)
    gram_ref[...] = prior[...] + gram if has_prior else gram

    def store(z, value):
        proj_ref[z] = value

    project(z_cells, group, rows, xf_ref, wide, proj, store)


def last_gram_kernel(z_cells, parts, n_y, n_z, plan, xf_ref, *refs):
    priors = len(plan) - 1
    pieces, refs = refs[:parts], refs[parts:]
    prior, refs = refs[0], refs[1:]
    prior_proj, refs = refs[:priors], refs[priors:]
    outs, (wide, proj, gram, full) = refs[:2], refs[2:]
    group, rows, _ = pieces[0].shape
    me, my_y, my_z = (lax.axis_index(a) for a in ("ga", "gy", "gz"))
    gather_rows(parts, me, pieces, wide)

    def place(z, value, segments):
        at = 0
        for first, count in segments:
            y_count = count // z_cells
            full[z, first // z_cells : first // z_cells + y_count, :] = value[at : at + y_count]
            at += y_count

    project(z_cells, group, rows, xf_ref, wide, proj, lambda z, value: place(z, value, plan[-1]))
    for i in range(priors):
        for z in range(z_cells):
            place(z, prior_proj[i][z], plan[i])
    data = wide[...]
    gram[...] = prior[...] + lax.dot_general(
        data, data, (((0,), (0,)), ((), ())), preferred_element_type=f32
    )
    own = gram.shape[0] // (n_y * n_z)
    width = gram.shape[1]
    layers = z_cells // n_y
    cols = full.shape[2]
    y_cells = full.shape[1]
    for flip, out in enumerate(outs):
        out[...] = jnp.zeros_like(out)
        for d_x in range(n_y // 2):
            for d_z in range(n_z):
                block = d_x * n_z + d_z
                y_to, z_to = my_y ^ (2 * d_x + flip), my_z ^ d_z
                at = pl.multiple_of((y_to * n_z + z_to) * own, own)
                out[block, :own, :width] = gram[pl.ds(at, own), :].astype(bf16)
                if d_z == 0:
                    for layer in range(layers):
                        out[block, :y_cells, width + layer * cols : width + (layer + 1) * cols] = full[
                            y_to * layers + layer
                        ]


def pair_kernel(n_z, own, y_cells, width, keep_ref, other_ref, *outs):
    blocks = keep_ref.shape[0]
    side = keep_ref.shape[2] - width
    for block in range(blocks):
        if block % n_z == 0:
            out = outs[blocks + block // n_z]
            out[:, :side] = keep_ref[block, :y_cells, width:]
            out[:, side:] = other_ref[block, :y_cells, width:]
    for block in range(blocks):
        both = keep_ref[block, :own, :width].astype(f32) + other_ref[block, :own, :width].astype(f32)
        outs[block][...] = both.astype(bf16)


def layer_kernel(n_y, paired, layers, y_scale, yf_ref, *refs):
    pieces, (out_ref, m_ref) = refs[:-2], refs[-2:]
    _, y_size = yf_ref.shape
    y_cells = y_size // n_y
    cols = m_ref.shape[2]
    senders = 2 if paired else 1
    my_y = lax.axis_index("gy")
    for d, piece in enumerate(pieces):
        for sender in range(senders):
            source = my_y ^ (2 * d + sender) if paired else origin(n_y, my_y, d)
            at = pl.multiple_of(source * y_cells, y_cells)
            for layer in range(layers):
                start = (sender * layers + layer) * cols
                m_ref[layer, pl.ds(at, y_cells), :] = piece[:, start : start + cols]
    for layer in range(layers):
        m = m_ref[layer]
        y_gram = lax.dot_general(m, m, (((1,), (1,)), ((), ())), preferred_element_type=f32) * y_scale
        prod = lax.dot_general(
            yf_ref[...], y_gram, (((1,), (0,)), ((), ())), preferred_element_type=f32,
            precision=lax.Precision.HIGHEST,
        )
        out_ref[:, layer * y_size : (layer + 1) * y_size] = prod.astype(bf16)


def total_of(pieces):
    total = pieces[0][...].astype(f32)
    for piece in pieces[1:]:
        total = total + piece[...].astype(f32)
    return total


def sum_kernel(scale, after, *refs):
    refs[-1][...] = (total_of(refs[:-1]) * scale).astype(bf16)


def mark_kernel(value_ref, out_ref):
    out_ref[...] = value_ref[:16, :128]


def last_kernel(parts, *refs):
    grams, prods, (gram_ref, prod_ref) = refs[:parts], refs[parts : 2 * parts], refs[2 * parts :]
    total = total_of(prods)
    layers, _, y_size = prod_ref.shape
    for layer in range(layers):
        prod_ref[layer] = total[:, layer * y_size : (layer + 1) * y_size]
    gram_ref[...] = total_of(grams)


def call(kernel, out_shapes, in_specs, scratch=(), limit=16, flops=0, moved=0):
    return pl.pallas_call(
        kernel,
        out_shape=out_shapes,
        in_specs=in_specs,
        out_specs=[VMEM] * len(out_shapes),
        scratch_shapes=list(scratch),
        cost_estimate=pl.CostEstimate(flops=flops, bytes_accessed=moved, transcendentals=0),
        compiler_params=pltpu.CompilerParams(vmem_limit_bytes=limit * MIB),
    )


def shards(fields, section_start, velocity, diffusivity, reaction, x_factor, y_factor):
    variables, y_cells, z_cells, lanes = fields.shape
    rows = y_cells * z_cells
    n_y, n_z, n_a = (lax.axis_size(a) for a in ("gy", "gz", "ga"))
    g_y, _, _ = (lax.axis_index(a) for a in ("gy", "gz", "ga"))
    f = fields.reshape(variables, rows, lanes)
    s = section_start.reshape(variables, rows, lanes)
    vel = velocity.reshape(3, rows, lanes)
    x_size = n_a * lanes
    y_size = n_y * y_cells
    rank, y_rank = x_factor.shape[1], y_factor.shape[1]
    group = variables // n_a
    owners = n_y * n_z
    own = x_size // owners
    layers = z_cells // n_y
    pad = -(-z_cells // 8) * 8
    tile = TILE
    quarter = rows // 4
    plan = (((quarter, 2 * quarter),), ((0, quarter), (3 * quarter, quarter)))
    chunk = 2 * quarter
    y_part = chunk // z_cells
    counts = (n_y, n_z, n_a)
    in_hbm = functools.partial(pltpu.with_memory_space_constraint, memory_space=pltpu.HBM)
    packed = call(
        functools.partial(pack_kernel, z_cells, counts, plan),
        [sds((variables, rows, lanes), f32)]
        + [sds((variables, z_cells, lanes), f32)] * turns(n_y)
        + [sds((len(plan), variables * chunk), f32)] * turns(n_a)
        + [sds((variables, y_part, lanes), bf16)] * (turns(n_z) * len(plan)),
        [ANY],
        scratch=[pltpu.SemaphoreType.DMA((min(variables, 8),))],
        limit=12,
    )(in_hbm(f))
    f, packed = packed[0], packed[1:]
    y_faces, packed = packed[: turns(n_y)], packed[turns(n_y) :]
    x_edges, z_faces = packed[: turns(n_a)], packed[turns(n_a) :]

    def halo(axis, count, faces):
        received = []
        for turn, face in enumerate(faces):
            received.append(lax.ppermute(face, axis, swap_pairs(count, turn)))
        return received

    mix, vel = call(
        mix_kernel,
        [sds((variables * SUB, variables * SUB), bf16), sds(vel.shape, f32)],
        [VMEM, ANY, ANY],
        scratch=[pltpu.SemaphoreType.DMA],
        limit=8,
    )(reaction, in_hbm(vel), y_faces[0])

    def stencil(index, x_halos, z_halos, y_halos):
        segments = plan[index]
        operands = [diffusivity, vel, s, f, mix, *x_halos, *z_halos, *y_halos]
        return pl.pallas_call(
            functools.partial(stencil_kernel, z_cells, counts, index, segments, bool(y_halos)),
            out_shape=[sds((variables, chunk, lanes), f32)] + [sds((group, chunk, lanes), bf16)] * n_a,
            in_specs=[SMEM] + [VMEM] * (len(operands) - 1),
            out_specs=[VMEM] * (n_a + 1),
            scratch_shapes=[
                pltpu.VMEM((2, variables, tile + 2 * pad, lanes), f32),
                pltpu.VMEM((variables, chunk, lanes), f32),
                pltpu.VMEM((variables, chunk, lanes), f32),
                pltpu.VMEM((2, variables * SUB, tile // SUB * lanes), f32),
            ],
            name="stencil",
            compiler_params=pltpu.CompilerParams(vmem_limit_bytes=20 * MIB),
        )(*operands)

    def exchange(snaps):
        received = [snaps[0]]
        for k in range(1, n_a):
            received.append(lax.ppermute(snaps[k], "ga", ring_pairs(n_a, k)))
        return received

    early_z, late_z = z_faces[: turns(n_z)], z_faces[turns(n_z) :]
    z_halos = halo("gz", n_z, early_z)
    x_halos = halo("ga", n_a, x_edges)
    y_halos = halo("gy", n_y, y_faces)
    results = stencil(0, x_halos, z_halos, ())
    news = [results[0]]
    chunks = [exchange(results[1:])]
    late_z, _ = lax.optimization_barrier((tuple(late_z), results[2]))
    z_halos = halo("gz", n_z, late_z)
    results = stencil(1, x_halos, z_halos, y_halos)
    news.append(results[0])
    chunks.append(exchange(results[1:]))
    new_fields = pl.pallas_call(
        functools.partial(flush_kernel, plan),
        out_shape=sds((variables, rows, lanes), f32),
        in_specs=[VMEM] * len(plan),
        out_specs=ANY,
        scratch_shapes=[pltpu.SemaphoreType.DMA((sum(len(segments) for segments in plan),))],
        name="flush",
        compiler_params=pltpu.CompilerParams(vmem_limit_bytes=4 * MIB),
    )(*news)

    scratch = [pltpu.VMEM((group * chunk, x_size), bf16), pltpu.VMEM((group * chunk, rank), f32)]
    gram, projs = None, []
    direct = owners <= 8 and n_y in (2, 4, 8) and n_z in (1, 2, 4)
    for index in range(len(plan) - 1 if direct else len(plan)):
        gram, proj = call(
            functools.partial(part_gram_kernel, z_cells, n_a, gram is not None),
            [sds((x_size, x_size), f32), sds((z_cells, y_part, group * rank), bf16)],
            [VMEM] * (n_a + 1 + (gram is not None)),
            scratch=scratch,
        )(x_factor.T, *chunks[index], *([] if gram is None else [gram]))
        projs.append(proj)
    cols = layers * group * rank
    piece_rows = max(own, y_cells)
    if direct:
        blocks = n_y // 2 * n_z
        keep, send = call(
            functools.partial(last_gram_kernel, z_cells, n_a, n_y, n_z, plan),
            [sds((blocks, piece_rows, x_size + cols), bf16)] * 2,
            [VMEM] * (n_a + 2 + len(projs)),
            scratch=scratch
            + [pltpu.VMEM((x_size, x_size), f32), pltpu.VMEM((z_cells, y_cells, group * rank), bf16)],
        )(x_factor.T, *chunks[-1], gram, *projs)
        other = lax.ppermute(send, "gy", swap_pairs(n_y, 0))
        sums = call(
            functools.partial(pair_kernel, n_z, own, y_cells, x_size),
            [sds((own, x_size), bf16)] * blocks + [sds((y_cells, 2 * cols), bf16)] * (n_y // 2),
            [VMEM] * 2,
        )(keep, other)
        sums, sides = sums[:blocks], sums[blocks:]
        side_parts = [sides[0]]
        for d_x in range(1, n_y // 2):
            side_parts.append(lax.ppermute(sides[d_x], "gy", [(y, y ^ (2 * d_x)) for y in range(n_y)]))
        received = [sums[0]]
        for block in range(1, blocks):
            d_x, d_z = block // n_z, block % n_z
            pairs = [
                (y * n_z + z, (y ^ (2 * d_x)) * n_z + (z ^ d_z)) for y in range(n_y) for z in range(n_z)
            ]
            received.append(lax.ppermute(sums[block], ("gy", "gz"), pairs))
    else:
        half = quarter // z_cells
        proj = jnp.concatenate([projs[1][:, :half], projs[0], projs[1][:, half:]], axis=1)
        full = lax.all_to_all(
            proj.reshape(n_y, layers, y_cells, group * rank), "gy", split_axis=0, concat_axis=0, tiled=True
        )
        blocks = lax.all_to_all(
            gram.astype(bf16).reshape(owners, own, x_size), ("gy", "gz"), split_axis=0, concat_axis=0, tiled=True
        )
        full = full.transpose(0, 2, 1, 3).reshape(n_y, y_cells, cols)
        received = list(blocks)
        side_parts = [
            lax.dynamic_index_in_dim(full, origin(n_y, g_y, d_y), 0, keepdims=False) for d_y in range(n_y)
        ]
    prods = call(
        functools.partial(layer_kernel, n_y, direct, layers, 1.0 / (variables * rank)),
        [sds((y_rank, layers * y_size), bf16)],
        [VMEM] * (1 + len(side_parts)),
        scratch=[pltpu.VMEM((layers, y_size, group * rank), bf16)],
    )(y_factor.T, *side_parts)[0]
    mark = call(mark_kernel, [sds((16, 128), bf16)], [VMEM], limit=2)(prods)[0]
    gram = call(
        functools.partial(sum_kernel, 1.0 / (variables * rows * owners)),
        [sds((own, x_size), bf16)],
        [ANY] + [VMEM] * len(received),
    )(mark, *received)[0]

    def spread(value):
        values = [value]
        for k in range(1, n_a):
            values.append(lax.ppermute(value, "ga", [(i, partner(n_a, i, k)) for i in range(n_a)]))
        return values

    x_gram, products = call(
        functools.partial(last_kernel, n_a),
        [sds((own, x_size), f32), sds((layers, y_rank, y_size), f32)],
        [VMEM] * (2 * n_a),
        limit=8,
    )(*spread(gram), *spread(prods))
    return (
        new_fields.reshape(fields.shape),
        x_gram,
        jnp.swapaxes(products, 1, 2),
    )


def solution(mesh):
    block = P(None, "gy", "gz", "ga")
    in_specs = (block, block, block, P(), P(), P(), P())
    out_specs = (block, P(("gy", "gz"), None), P(("gz", "gy"), None, None))

    return jax.shard_map(shards, mesh=mesh, in_specs=in_specs, out_specs=out_specs, check_vma=False)
```

```python
import functools

import jax
import jax.numpy as jnp
from jax import lax
from jax.experimental import pallas as pl
from jax.experimental.pallas import tpu as pltpu
from jax.sharding import PartitionSpec as P


time_step = 0.4
old_share, new_share = 0.75, 0.25
TILE = 32
SUB = 16
VMEM = pl.BlockSpec(memory_space=pltpu.VMEM)
SMEM = pl.BlockSpec(memory_space=pltpu.SMEM)
ANY = pl.BlockSpec(memory_space=pl.ANY)
f32, bf16 = jnp.float32, jnp.bfloat16
sds = jax.ShapeDtypeStruct
MIB = 1024 * 1024


def swap_pairs(count, turn):
    if turn == 0:
        return [(i, i ^ 1) for i in range(count)]
    return [(i, (i + (1 if i % 2 else -1)) % count) for i in range(count)]


def partner(count, index, step):
    if count & (count - 1) == 0:
        return index ^ step
    return (index + step) % count


def origin(count, index, step):
    if count & (count - 1) == 0:
        return index ^ step
    return (index - step + count) % count


def turns(count):
    return 1 if count == 2 else 2


def ring_pairs(count, step):
    return [(i, (i + step) % count) for i in range(count)]


def corner_mask(lanes):
    row = lax.broadcasted_iota(jnp.int32, (8, lanes), 0)
    lane = lax.broadcasted_iota(jnp.int32, (8, lanes), 1)
    return jnp.where(
        ((row == 0) & (lane == 0)) | ((row == 1) & (lane == lanes - 1)), 1.0, 0.0
    ).astype(bf16)


def rows_of(ref, v, segments):
    return jnp.concatenate([ref[v, first : first + count, :] for first, count in segments], axis=0)


def pack_kernel(z_cells, counts, plan, f_hbm, *refs):
    f_ref, outs, sem = refs[0], refs[1:-1], refs[-1]
    variables, rows, lanes = f_ref.shape
    n_y, n_z, n_a = counts
    n_sem = sem.shape[0]
    step = variables // n_sem
    loads = [
        pltpu.make_async_copy(
            f_hbm.at[pl.ds(i * step, step)], f_ref.at[pl.ds(i * step, step)], sem.at[i]
        )
        for i in range(n_sem)
    ]
    for load in loads:
        load.start()
    y_refs, outs = outs[: turns(n_y)], outs[turns(n_y) :]
    x_refs, z_refs = outs[: turns(n_a)], outs[turns(n_a) :]
    odd_y, odd_z, odd_a = (lax.rem(lax.axis_index(a), 2) for a in ("gy", "gz", "ga"))
    pick = corner_mask(lanes)
    for v in range(variables):
        if v % step == 0:
            loads[v // step].wait()
        for c, segments in enumerate(plan):
            size = sum(count for _, count in segments)
            at = 0
            for first, count in segments:
                y_count = count // z_cells
                for turn in range(turns(n_z)):
                    start = first + jnp.where(odd_z == turn, z_cells - 1, 0)
                    z_refs[c * turns(n_z) + turn][v, at : at + y_count, :] = f_ref[
                        v, pl.ds(start, y_count, stride=z_cells), :
                    ].astype(bf16)
                at += y_count
            edges = lax.dot_general(
                pick, rows_of(f_ref, v, segments).astype(bf16), (((1,), (1,)), ((), ())),
                preferred_element_type=f32,
            )
            for turn in range(turns(n_a)):
                x_refs[turn][c : c + 1, v * size : (v + 1) * size] = jnp.where(
                    odd_a == turn, edges[1:2, :], edges[0:1, :]
                )
        for turn in range(turns(n_y)):
            y_refs[turn][v] = jnp.where(
                odd_y == turn, f_ref[v, rows - z_cells :, :], f_ref[v, :z_cells, :]
            )


def low_high(axis, count, halos):
    index = lax.axis_index(axis)
    odd = lax.rem(index, 2)
    a, b = halos[0], halos[-1]

    def pick(value_of):
        first, second = value_of(a), value_of(b)
        low = jnp.where(odd == 1, first, second)
        high = jnp.where(odd == 1, second, first)
        zero = jnp.zeros_like(low)
        return jnp.where(index > 0, low, zero), jnp.where(index < count - 1, high, zero)

    return pick


def mix_kernel(r_ref, vel_hbm, f_ref, out_ref, vel_ref, sem):
    load = pltpu.make_async_copy(vel_hbm, vel_ref, sem)
    load.start()
    count = r_ref.shape[0]
    size = out_ref.shape[1]
    spread = jnp.where(
        lax.broadcasted_iota(jnp.int32, (size, count), 0) // SUB
        == lax.broadcasted_iota(jnp.int32, (size, count), 1),
        1.0,
        0.0,
    ).astype(bf16)
    scaled = (r_ref[...] * (new_share * time_step)).astype(bf16)
    left = lax.dot_general(spread, scaled, (((1,), (0,)), ((), ())), preferred_element_type=f32)
    both = lax.dot_general(
        left.astype(bf16), spread, (((1,), (1,)), ((), ())), preferred_element_type=f32
    )
    row = lax.broadcasted_iota(jnp.int32, (size, size), 0)
    col = lax.broadcasted_iota(jnp.int32, (size, size), 1)
    mix = jnp.where(row % SUB == col % SUB, both, 0.0).astype(bf16)
    for t in range(out_ref.shape[0]):
        blocks = []
        for at in range(t * TILE, (t + 1) * TILE, SUB):
            blocks.append(
                jnp.concatenate([f_ref[w, at : at + SUB, :].astype(bf16) for w in range(count)], axis=0)
            )
        out_ref[t] = jnp.dot(mix, jnp.concatenate(blocks, axis=1), preferred_element_type=f32)
    load.wait()


def stencil_kernel(
    z_cells, counts, index, segments, chosen, has_y, diffusion, vel_ref, start_ref, f_ref, react, *rest
):
    n_y, n_z, parts = counts
    x_refs, rest = rest[: turns(parts)], rest[turns(parts) :]
    z_refs, rest = rest[: turns(n_z)], rest[turns(n_z) :]
    if has_y:
        y_refs, rest = rest[: turns(n_y)], rest[turns(n_y) :]
    many = len(chosen)
    news, snaps, (ends, edge, zface) = rest[:many], rest[many : 2 * many], rest[2 * many :]
    variables, rows, lanes = f_ref.shape
    pad = -(-z_cells // 8) * 8
    tile = TILE
    group = variables // parts
    chunk = sum(count for _, count in segments)
    me = lax.axis_index("ga")
    is_buffer = me == parts - 1
    tile_rows = [first + k * tile for first, count in segments for k in range(count // tile)]
    picked = []
    for i, part in enumerate(chosen):
        target = lax.rem(me + part, parts)
        picked += [(i, j, target * group + j) for j in range(group)]

    put = corner_mask(lanes)
    side = lax.broadcasted_iota(jnp.int32, (8, chunk), 0)
    y_count = chunk // z_cells
    x_pair = low_high("ga", parts, x_refs)
    z_pair = low_high("gz", n_z, z_refs)
    for slot, (_, _, v) in enumerate(picked):
        at = pl.ds(pl.multiple_of(v * chunk, 128), chunk)
        first, second = x_pair(lambda ref: ref[index : index + 1, at])
        first = jnp.broadcast_to(first, (8, chunk))
        second = jnp.broadcast_to(second, (8, chunk))
        both = jnp.where(side == 0, first, jnp.where(side == 1, second, 0.0)).astype(bf16)
        edge[slot] = lax.dot_general(both, put, (((0,), (0,)), ((), ())), preferred_element_type=f32)
        first, second = z_pair(lambda ref: ref[v].astype(f32))
        zface[slot, pl.ds(0, y_count, stride=z_cells), :] = first
        zface[slot, pl.ds(z_cells - 1, y_count, stride=z_cells), :] = second
    if has_y:
        low, high = low_high("gy", n_y, y_refs)(lambda ref: ref[...])
        ends[0, :, pad - z_cells : pad, :] = low
        ends[0, :, pad:, :] = f_ref[:, : tile + pad, :]
        ends[1, :, : tile + pad, :] = f_ref[:, rows - tile - pad :, :]
        ends[1, :, tile + pad : tile + pad + z_cells, :] = high

    rate = new_share * time_step
    lane = lax.broadcasted_iota(jnp.int32, (SUB, lanes), 1)
    z_at = lax.rem(lax.broadcasted_iota(jnp.int32, (SUB, lanes), 0), z_cells)
    for t, row in enumerate(tile_rows):
        for sub in range(tile // SUB):
            at, here = row + sub * SUB, t * tile + sub * SUB

            def rows_at(v, offset):
                if row == 0:
                    return ends[0, v, pad + sub * SUB + offset : pad + (sub + 1) * SUB + offset, :]
                if row == rows - tile:
                    return ends[1, v, pad + sub * SUB + offset : pad + (sub + 1) * SUB + offset, :]
                return f_ref[v, at + offset : at + SUB + offset, :]

            v_x = vel_ref[0, at : at + SUB, :] * (0.5 * rate)
            v_y = vel_ref[1, at : at + SUB, :] * (0.5 * rate)
            v_z = vel_ref[2, at : at + SUB, :] * (0.5 * rate)
            for slot, (i, j, v) in enumerate(picked):
                spread = diffusion[v] * rate
                center = rows_at(v, 0)
                y_minus = rows_at(v, -z_cells)
                y_plus = rows_at(v, z_cells)
                face = zface[slot, here : here + SUB, :]
                z_minus = jnp.where(z_at == 0, face, rows_at(v, -1))
                z_plus = jnp.where(z_at == z_cells - 1, face, rows_at(v, 1))
                sides = edge[slot, here : here + SUB, :]
                x_minus = jnp.where(lane == 0, sides, pltpu.roll(center, 1, 1))
                x_plus = jnp.where(lane == lanes - 1, sides, pltpu.roll(center, lanes - 1, 1))
                mixed = react[
                    row // tile, pl.ds(pl.multiple_of(v * SUB, SUB), SUB), sub * lanes : (sub + 1) * lanes
                ]
                around = (y_plus + y_minus) + (z_plus + z_minus) + (x_plus + x_minus)
                carried = v_x * (x_plus - x_minus) + v_y * (y_plus - y_minus) + v_z * (z_plus - z_minus)
                value = (
                    old_share * start_ref[v, at : at + SUB, :]
                    + (new_share - 6.0 * spread) * center
                    + (spread * around - carried)
                    + mixed
                )
                value = jnp.where(is_buffer, center, value)
                news[i][j, here : here + SUB, :] = value
                snaps[i][j, here : here + SUB, :] = value.astype(bf16)


def flush_kernel(plan, parts, *refs):
    news, (new_hbm, sem) = refs[:-2], refs[-2:]
    me = lax.axis_index("ga")
    writes = []
    for c, segments in enumerate(plan):
        for part in range(parts):
            ref = news[c * parts + part]
            group = ref.shape[0]
            to = pl.ds(lax.rem(me + part, parts) * group, group)
            at = 0
            for first, count in segments:
                writes.append(
                    pltpu.make_async_copy(
                        ref.at[:, pl.ds(at, count), :],
                        new_hbm.at[to, pl.ds(first, count), :],
                        sem.at[len(writes)],
                    )
                )
                writes[-1].start()
                at += count
    for write in writes:
        write.wait()


def gather_rows(parts, me, pieces, wide):
    group, rows, lanes = pieces[0].shape
    for part in range(parts):
        source = lax.rem(me - part + parts, parts)
        at = pl.multiple_of(source * lanes, lanes)
        for j in range(group):
            wide[j * rows : (j + 1) * rows, pl.ds(at, lanes)] = pieces[part][j]


def project(z_cells, group, rows, xf_ref, wide, proj, store):
    y_cells = rows // z_cells
    proj[...] = lax.dot_general(
        wide[...], xf_ref[...], (((1,), (1,)), ((), ())), preferred_element_type=f32
    )
    for z in range(z_cells):
        cols = [proj[pl.ds(j * rows + z, y_cells, stride=z_cells), :] for j in range(group)]
        store(z, jnp.concatenate(cols, axis=1).astype(bf16))


def part_gram_kernel(z_cells, parts, has_prior, xf_ref, *refs):
    pieces, refs = refs[:parts], refs[parts:]
    if has_prior:
        prior, refs = refs[0], refs[1:]
    gram_ref, proj_ref, wide, proj = refs
    group, rows, _ = pieces[0].shape
    gather_rows(parts, lax.axis_index("ga"), pieces, wide)
    data = wide[...]
    gram = lax.dot_general(data, data, (((0,), (0,)), ((), ())), preferred_element_type=f32)
    gram_ref[...] = prior[...] + gram if has_prior else gram

    def store(z, value):
        proj_ref[z] = value

    project(z_cells, group, rows, xf_ref, wide, proj, store)


def last_gram_kernel(z_cells, parts, n_y, n_z, plan, xf_ref, *refs):
    priors = len(plan) - 1
    pieces, refs = refs[:parts], refs[parts:]
    prior, refs = refs[0], refs[1:]
    prior_proj, refs = refs[:priors], refs[priors:]
    outs, (wide, proj, gram, full) = refs[:2], refs[2:]
    group, rows, _ = pieces[0].shape
    me, my_y, my_z = (lax.axis_index(a) for a in ("ga", "gy", "gz"))
    gather_rows(parts, me, pieces, wide)

    def place(z, value, segments):
        at = 0
        for first, count in segments:
            y_count = count // z_cells
            full[z, first // z_cells : first // z_cells + y_count, :] = value[at : at + y_count]
            at += y_count

    project(z_cells, group, rows, xf_ref, wide, proj, lambda z, value: place(z, value, plan[-1]))
    for i in range(priors):
        for z in range(z_cells):
            place(z, prior_proj[i][z], plan[i])
    data = wide[...]
    gram[...] = prior[...] + lax.dot_general(
        data, data, (((0,), (0,)), ((), ())), preferred_element_type=f32
    )
    own = gram.shape[0] // (n_y * n_z)
    width = gram.shape[1]
    layers = z_cells // n_y
    cols = full.shape[2]
    y_cells = full.shape[1]
    for flip, out in enumerate(outs):
        out[...] = jnp.zeros_like(out)
        for d_x in range(n_y // 2):
            for d_z in range(n_z):
                block = d_x * n_z + d_z
                y_to, z_to = my_y ^ (2 * d_x + flip), my_z ^ d_z
                at = pl.multiple_of((y_to * n_z + z_to) * own, own)
                out[block, :own, :width] = gram[pl.ds(at, own), :].astype(bf16)
                if d_z == 0:
                    for layer in range(layers):
                        out[block, :y_cells, width + layer * cols : width + (layer + 1) * cols] = full[
                            y_to * layers + layer
                        ]


def pair_kernel(n_z, own, y_cells, width, keep_ref, other_ref, *outs):
    blocks = keep_ref.shape[0]
    side = keep_ref.shape[2] - width
    for block in range(blocks):
        if block % n_z == 0:
            out = outs[blocks + block // n_z]
            out[:, :side] = keep_ref[block, :y_cells, width:]
            out[:, side:] = other_ref[block, :y_cells, width:]
    for block in range(blocks):
        both = keep_ref[block, :own, :width].astype(f32) + other_ref[block, :own, :width].astype(f32)
        outs[block][...] = both.astype(bf16)


def layer_kernel(n_y, paired, layers, y_scale, yf_ref, *refs):
    pieces, (out_ref, m_ref) = refs[:-2], refs[-2:]
    _, y_size = yf_ref.shape
    y_cells = y_size // n_y
    cols = m_ref.shape[2]
    senders = 2 if paired else 1
    my_y = lax.axis_index("gy")
    for d, piece in enumerate(pieces):
        for sender in range(senders):
            source = my_y ^ (2 * d + sender) if paired else origin(n_y, my_y, d)
            at = pl.multiple_of(source * y_cells, y_cells)
            for layer in range(layers):
                start = (sender * layers + layer) * cols
                m_ref[layer, pl.ds(at, y_cells), :] = piece[:, start : start + cols]
    for layer in range(layers):
        m = m_ref[layer]
        y_gram = lax.dot_general(m, m, (((1,), (1,)), ((), ())), preferred_element_type=f32) * y_scale
        prod = lax.dot_general(
            yf_ref[...], y_gram, (((1,), (0,)), ((), ())), preferred_element_type=f32,
            precision=lax.Precision.HIGHEST,
        )
        out_ref[:, layer * y_size : (layer + 1) * y_size] = prod.astype(bf16)


def total_of(pieces):
    total = pieces[0][...].astype(f32)
    for piece in pieces[1:]:
        total = total + piece[...].astype(f32)
    return total


def sum_kernel(scale, after, *refs):
    refs[-1][...] = (total_of(refs[:-1]) * scale).astype(bf16)


def mark_kernel(value_ref, out_ref):
    out_ref[...] = value_ref[:16, :128]


def last_kernel(parts, *refs):
    grams, prods, (gram_ref, prod_ref) = refs[:parts], refs[parts : 2 * parts], refs[2 * parts :]
    total = total_of(prods)
    layers, _, y_size = prod_ref.shape
    for layer in range(layers):
        prod_ref[layer] = total[:, layer * y_size : (layer + 1) * y_size]
    gram_ref[...] = total_of(grams)


def call(kernel, out_shapes, in_specs, scratch=(), limit=16, flops=0, moved=0):
    return pl.pallas_call(
        kernel,
        out_shape=out_shapes,
        in_specs=in_specs,
        out_specs=[VMEM] * len(out_shapes),
        scratch_shapes=list(scratch),
        cost_estimate=pl.CostEstimate(flops=flops, bytes_accessed=moved, transcendentals=0),
        compiler_params=pltpu.CompilerParams(vmem_limit_bytes=limit * MIB),
    )


def shards(fields, section_start, velocity, diffusivity, reaction, x_factor, y_factor):
    variables, y_cells, z_cells, lanes = fields.shape
    rows = y_cells * z_cells
    n_y, n_z, n_a = (lax.axis_size(a) for a in ("gy", "gz", "ga"))
    g_y, _, _ = (lax.axis_index(a) for a in ("gy", "gz", "ga"))
    f = fields.reshape(variables, rows, lanes)
    s = section_start.reshape(variables, rows, lanes)
    vel = velocity.reshape(3, rows, lanes)
    x_size = n_a * lanes
    y_size = n_y * y_cells
    rank, y_rank = x_factor.shape[1], y_factor.shape[1]
    group = variables // n_a
    owners = n_y * n_z
    own = x_size // owners
    layers = z_cells // n_y
    pad = -(-z_cells // 8) * 8
    tile = TILE
    quarter = rows // 4
    plan = (((quarter, 2 * quarter),), ((0, quarter), (3 * quarter, quarter)))
    chunk = 2 * quarter
    y_part = chunk // z_cells
    counts = (n_y, n_z, n_a)
    in_hbm = functools.partial(pltpu.with_memory_space_constraint, memory_space=pltpu.HBM)
    packed = call(
        functools.partial(pack_kernel, z_cells, counts, plan),
        [sds((variables, rows, lanes), f32)]
        + [sds((variables, z_cells, lanes), f32)] * turns(n_y)
        + [sds((len(plan), variables * chunk), f32)] * turns(n_a)
        + [sds((variables, y_part, lanes), bf16)] * (turns(n_z) * len(plan)),
        [ANY],
        scratch=[pltpu.SemaphoreType.DMA((min(variables, 8),))],
        limit=12,
    )(in_hbm(f))
    f, packed = packed[0], packed[1:]
    y_faces, packed = packed[: turns(n_y)], packed[turns(n_y) :]
    x_edges, z_faces = packed[: turns(n_a)], packed[turns(n_a) :]

    def halo(axis, count, faces):
        received = []
        for turn, face in enumerate(faces):
            received.append(lax.ppermute(face, axis, swap_pairs(count, turn)))
        return received

    react, vel = call(
        mix_kernel,
        [sds((rows // tile, variables * SUB, tile // SUB * lanes), f32), sds(vel.shape, f32)],
        [VMEM, ANY, VMEM],
        scratch=[pltpu.SemaphoreType.DMA],
        limit=12,
    )(reaction, in_hbm(vel), f)

    def stencil(index, chosen, x_halos, z_halos, y_halos):
        operands = [diffusivity, vel, s, f, react, *x_halos, *z_halos, *y_halos]
        many = len(chosen)
        results = pl.pallas_call(
            functools.partial(stencil_kernel, z_cells, counts, index, plan[index], chosen, bool(y_halos)),
            out_shape=[sds((group, chunk, lanes), f32)] * many + [sds((group, chunk, lanes), bf16)] * many,
            in_specs=[SMEM] + [VMEM] * (len(operands) - 1),
            out_specs=[VMEM] * (2 * many),
            scratch_shapes=[
                pltpu.VMEM((2, variables, tile + 2 * pad, lanes), f32),
                pltpu.VMEM((many * group, chunk, lanes), f32),
                pltpu.VMEM((many * group, chunk, lanes), f32),
            ],
            name="stencil",
            compiler_params=pltpu.CompilerParams(vmem_limit_bytes=20 * MIB),
        )(*operands)
        return list(results[:many]), list(results[many:])

    def exchange(snaps):
        received = [snaps[0]]
        for k in range(1, n_a):
            received.append(lax.ppermute(snaps[k], "ga", ring_pairs(n_a, k)))
        return received

    early_z, late_z = z_faces[: turns(n_z)], z_faces[turns(n_z) :]
    z_halos = halo("gz", n_z, early_z)
    x_halos = halo("ga", n_a, x_edges)
    y_halos = halo("gy", n_y, y_faces)
    head_news, head = stencil(0, (1,), x_halos, z_halos, ())
    others = (0,) + tuple(range(2, n_a))
    rest_news, rest = stencil(0, others, x_halos, z_halos, ())
    news = rest_news[:1] + head_news + rest_news[1:]
    chunks = [exchange(rest[:1] + head + rest[1:])]
    late_z, _ = lax.optimization_barrier((tuple(late_z), head[0]))
    z_halos = halo("gz", n_z, late_z)
    more, snaps = stencil(1, tuple(range(n_a)), x_halos, z_halos, y_halos)
    news += more
    chunks.append(exchange(snaps))
    new_fields = pl.pallas_call(
        functools.partial(flush_kernel, plan, n_a),
        out_shape=sds((variables, rows, lanes), f32),
        in_specs=[VMEM] * len(news),
        out_specs=ANY,
        scratch_shapes=[pltpu.SemaphoreType.DMA((n_a * sum(len(segments) for segments in plan),))],
        name="flush",
        compiler_params=pltpu.CompilerParams(vmem_limit_bytes=4 * MIB),
    )(*news)

    scratch = [pltpu.VMEM((group * chunk, x_size), bf16), pltpu.VMEM((group * chunk, rank), f32)]
    gram, projs = None, []
    direct = owners <= 8 and n_y in (2, 4, 8) and n_z in (1, 2, 4)
    for index in range(len(plan) - 1 if direct else len(plan)):
        gram, proj = call(
            functools.partial(part_gram_kernel, z_cells, n_a, gram is not None),
            [sds((x_size, x_size), f32), sds((z_cells, y_part, group * rank), bf16)],
            [VMEM] * (n_a + 1 + (gram is not None)),
            scratch=scratch,
        )(x_factor.T, *chunks[index], *([] if gram is None else [gram]))
        projs.append(proj)
    cols = layers * group * rank
    piece_rows = max(own, y_cells)
    if direct:
        blocks = n_y // 2 * n_z
        keep, send = call(
            functools.partial(last_gram_kernel, z_cells, n_a, n_y, n_z, plan),
            [sds((blocks, piece_rows, x_size + cols), bf16)] * 2,
            [VMEM] * (n_a + 2 + len(projs)),
            scratch=scratch
            + [pltpu.VMEM((x_size, x_size), f32), pltpu.VMEM((z_cells, y_cells, group * rank), bf16)],
        )(x_factor.T, *chunks[-1], gram, *projs)
        other = lax.ppermute(send, "gy", swap_pairs(n_y, 0))
        sums = call(
            functools.partial(pair_kernel, n_z, own, y_cells, x_size),
            [sds((own, x_size), bf16)] * blocks + [sds((y_cells, 2 * cols), bf16)] * (n_y // 2),
            [VMEM] * 2,
        )(keep, other)
        sums, sides = sums[:blocks], sums[blocks:]
        side_parts = [sides[0]]
        for d_x in range(1, n_y // 2):
            side_parts.append(lax.ppermute(sides[d_x], "gy", [(y, y ^ (2 * d_x)) for y in range(n_y)]))
        received = [sums[0]]
        for block in range(1, blocks):
            d_x, d_z = block // n_z, block % n_z
            pairs = [
                (y * n_z + z, (y ^ (2 * d_x)) * n_z + (z ^ d_z)) for y in range(n_y) for z in range(n_z)
            ]
            received.append(lax.ppermute(sums[block], ("gy", "gz"), pairs))
    else:
        half = quarter // z_cells
        proj = jnp.concatenate([projs[1][:, :half], projs[0], projs[1][:, half:]], axis=1)
        full = lax.all_to_all(
            proj.reshape(n_y, layers, y_cells, group * rank), "gy", split_axis=0, concat_axis=0, tiled=True
        )
        blocks = lax.all_to_all(
            gram.astype(bf16).reshape(owners, own, x_size), ("gy", "gz"), split_axis=0, concat_axis=0, tiled=True
        )
        full = full.transpose(0, 2, 1, 3).reshape(n_y, y_cells, cols)
        received = list(blocks)
        side_parts = [
            lax.dynamic_index_in_dim(full, origin(n_y, g_y, d_y), 0, keepdims=False) for d_y in range(n_y)
        ]
    prods = call(
        functools.partial(layer_kernel, n_y, direct, layers, 1.0 / (variables * rank)),
        [sds((y_rank, layers * y_size), bf16)],
        [VMEM] * (1 + len(side_parts)),
        scratch=[pltpu.VMEM((layers, y_size, group * rank), bf16)],
    )(y_factor.T, *side_parts)[0]
    mark = call(mark_kernel, [sds((16, 128), bf16)], [VMEM], limit=2)(prods)[0]
    gram = call(
        functools.partial(sum_kernel, 1.0 / (variables * rows * owners)),
        [sds((own, x_size), bf16)],
        [ANY] + [VMEM] * len(received),
    )(mark, *received)[0]

    def spread(value):
        values = [value]
        for k in range(1, n_a):
            values.append(lax.ppermute(value, "ga", [(i, partner(n_a, i, k)) for i in range(n_a)]))
        return values

    x_gram, products = call(
        functools.partial(last_kernel, n_a),
        [sds((own, x_size), f32), sds((layers, y_rank, y_size), f32)],
        [VMEM] * (2 * n_a),
        limit=8,
    )(*spread(gram), *spread(prods))
    return (
        new_fields.reshape(fields.shape),
        x_gram,
        jnp.swapaxes(products, 1, 2),
    )


def solution(mesh):
    block = P(None, "gy", "gz", "ga")
    in_specs = (block, block, block, P(), P(), P(), P())
    out_specs = (block, P(("gy", "gz"), None), P(("gz", "gy"), None, None))

    return jax.shard_map(shards, mesh=mesh, in_specs=in_specs, out_specs=out_specs, check_vma=False)
```
